512 devices in a mesh: lon: 32 (over z_lo, y), lat: 16 (over x, z_hi, core).
Axes of the slice: x: 4, y: 4, z: 16 (z_hi: 2, z_lo: 8; z = z_hi * 8 + z_lo), core: 2. Of those that a mesh axis runs over, the one named last changes fastest.
Arguments:
- heat_anomaly: float32 [75, 128, 4096], P(None, 'lat', 'lon'), may hold values from -6 to 6
- saltiness_anomaly: float32 [75, 128, 4096], P(None, 'lat', 'lon'), may hold values from -6 to 6
- zonal_edge_current: float32 [75, 128, 4096], P(None, 'lat', 'lon'), may hold values from -3 to 3
- meridional_edge_current: float32 [75, 128, 4096], P(None, 'lat', 'lon'), may hold values from -3 to 3
- interface_mixing_coefficient: float32 [74, 128, 4096], P(None, 'lat', 'lon'), may hold values from 0.05 to 5
- ocean_layer_number: int32 [128, 4096], P('lat', 'lon'), may hold values from 0 to 75, as said below
Outputs:
- heat_next: float32 [75, 128, 4096], P(None, 'lat', 'lon')
- saltiness_next: float32 [75, 128, 4096], P(None, 'lat', 'lon')
- zonal_current_next: float32 [75, 128, 4096], P(None, 'lat', 'lon')
- meridional_current_next: float32 [75, 128, 4096], P(None, 'lat', 'lon')
The draws below stay inside these ranges and needn't reach their ends.
Inputs may be any that keep to these rules, and one draw needn't show every extreme that they name: `ocean_layer_number`: 0 marks a land column.
All inputs are finite; a program needn't handle non-finite values.
Results may differ from the reference program's by a relative error of at most 0.0003.
Values sent between devices are 32-bit elements; how exact they have to be, the bound alone decides.
No kernel may reach another device: no remote copies, remote signals or barrier semaphores. Data moves between devices by JAX's collectives and lax.ppermute only.
A program may use at most 64 MiB of HBM per device.

```python
import math
import jax
import jax.numpy as jnp

SEA_LAYERS = 75
PARALLEL_POINTS = 4096
MERIDIAN_POINTS = 128


def draw_ocean_layer_number(key, part):
    subkeys = jax.random.split(key, 4)
    block_rows = (MERIDIAN_POINTS - 1) // 4 + 1
    block_cols = (PARALLEL_POINTS - 1) // 32 + 1
    block_depth = jax.random.randint(subkeys[0], (block_rows, block_cols), -(SEA_LAYERS // 2), SEA_LAYERS + SEA_LAYERS // 2)
    deep_row = jax.random.randint(subkeys[1], (), 0, block_rows)
    deep_col = jax.random.randint(subkeys[2], (), 0, block_cols)
    row_ids = jnp.arange(block_rows)[:, None]
    col_ids = jnp.arange(block_cols)[None, :]
    block_depth = jnp.where((row_ids == deep_row) & (col_ids == deep_col), SEA_LAYERS + 20, block_depth)
    block_depth = jnp.where((row_ids == deep_row) & (col_ids == (deep_col + 1) % block_cols), -SEA_LAYERS, block_depth)
    jitter = jax.random.randint(subkeys[3], (MERIDIAN_POINTS, PARALLEL_POINTS), -6, 7)
    column_depth = block_depth[jnp.arange(MERIDIAN_POINTS) // 4][:, jnp.arange(PARALLEL_POINTS) // 32]
    return jnp.clip(column_depth + jitter, 0, SEA_LAYERS).astype(jnp.int32)


def shard_levels(key, extent, cuts, low, high):
    loudness, own = 1.0, jax.random.fold_in(key, 6)
    for position, blocks in cuts:
        steps = jnp.exp(jax.random.uniform(jax.random.fold_in(own, position), (blocks,), jnp.float32, low / len(cuts), high / len(cuts)))
        loudness = loudness * jnp.repeat(steps, extent[position] // blocks).reshape([-1 if axis == position else 1 for axis in range(len(extent))])
    return loudness


def normal_values(stream_key, extent, spread, most, pieces=(), kind=jnp.bfloat16):
    gain = shard_levels(stream_key, extent, pieces, -0.22, 0.18) if pieces else 1.0
    drawn = jax.random.normal(stream_key, extent, jnp.float32) * spread * gain
    return jnp.minimum(jnp.maximum(drawn, -most), most).astype(kind)


def setup_inputs(seed: int = 0) -> dict:
    keys = jax.random.split(jax.random.key(seed), 7)
    heat_anomaly = normal_values(keys[0], (SEA_LAYERS, MERIDIAN_POINTS, PARALLEL_POINTS), 1.0, 6.0, ((1, 16), (2, 32)), jnp.float32)
    saltiness_anomaly = normal_values(keys[1], (SEA_LAYERS, MERIDIAN_POINTS, PARALLEL_POINTS), 1.0, 6.0, ((1, 16), (2, 32)), jnp.float32)
    zonal_edge_current = normal_values(keys[2], (SEA_LAYERS, MERIDIAN_POINTS, PARALLEL_POINTS), 0.5, 3.0, ((1, 16), (2, 32)), jnp.float32)
    meridional_edge_current = normal_values(keys[3], (SEA_LAYERS, MERIDIAN_POINTS, PARALLEL_POINTS), 0.5, 3.0, ((1, 16), (2, 32)), jnp.float32)
    interface_mixing_coefficient = jnp.clip(jnp.exp(math.log(5.0) - 4.6051702 * jax.random.uniform(keys[4], (SEA_LAYERS - 1, MERIDIAN_POINTS, PARALLEL_POINTS), jnp.float32) ** shard_levels(keys[4], (SEA_LAYERS - 1, MERIDIAN_POINTS, PARALLEL_POINTS), ((1, 16), (2, 32)), -0.2, 0.2)), 0.05, 5.0)
    ocean_layer_number = draw_ocean_layer_number(jax.random.fold_in(keys[6], 71), 0)
    return {"heat_anomaly": heat_anomaly, "saltiness_anomaly": saltiness_anomaly, "zonal_edge_current": zonal_edge_current, "meridional_edge_current": meridional_edge_current, "interface_mixing_coefficient": interface_mixing_coefficient, "ocean_layer_number": ocean_layer_number}


time_step = 0.2
diffusion = 0.5
viscosity = 0.5
vertical_viscosity = 0.5
pressure_coef = 0.05
coriolis_coef = 1.5
thermal_coef = 1.0
thermal_curve = 0.2
haline_coef = 0.8
cabbeling_coef = 0.1


def tendencies(heat_grid_values, salt_field, eastward, northward, depth_field, coriolis):
    layer_number = heat_grid_values.shape[0]
    heights = jnp.arange(layer_number, dtype=jnp.float32)[:, None, None] + 0.5
    ocean = (heights < depth_field[None]).astype(jnp.float32)
    density = ocean * (-thermal_coef * (1.0 + 0.5 * thermal_curve * heat_grid_values) * heat_grid_values
                       + haline_coef * salt_field - cabbeling_coef * heat_grid_values * salt_field)
    pressure = pressure_coef * (jnp.cumsum(density, axis=0) - 0.5 * density)
    east_open = ocean[:, 1:-1, :-1] * ocean[:, 1:-1, 1:]
    north_open = ocean[:, :-1, 1:-1] * ocean[:, 1:, 1:-1]
    ocean_mid = ocean[:, 1:-1, 1:-1]
    stars = []
    for tracer in (heat_grid_values, salt_field):
        flux_east = east_open * (eastward[:, 1:-1, :-1] * 0.5 * (tracer[:, 1:-1, :-1] + tracer[:, 1:-1, 1:])
                                 - diffusion * (tracer[:, 1:-1, 1:] - tracer[:, 1:-1, :-1]))
        flux_north = north_open * (northward[:, :-1, 1:-1] * 0.5 * (tracer[:, :-1, 1:-1] + tracer[:, 1:, 1:-1])
                                   - diffusion * (tracer[:, 1:, 1:-1] - tracer[:, :-1, 1:-1]))
        change = flux_east[:, :, 1:] - flux_east[:, :, :-1] + flux_north[:, 1:, :] - flux_north[:, :-1, :]
        stars.append(ocean_mid * (tracer[:, 1:-1, 1:-1] - time_step * change))
    east_mid = east_open[:, :, 1:]
    north_mid = north_open[:, 1:, :]
    zonal_mid = eastward[:, 1:-1, 1:-1]
    merid_mid = northward[:, 1:-1, 1:-1]
    north_avg = 0.25 * (merid_mid + northward[:, 1:-1, 2:] + northward[:, :-2, 1:-1] + northward[:, :-2, 2:])
    east_avg = 0.25 * (zonal_mid + eastward[:, 1:-1, :-2] + eastward[:, 2:, 1:-1] + eastward[:, 2:, :-2])
    zonal_laplacian = (eastward[:, 1:-1, 2:] + eastward[:, 1:-1, :-2] + eastward[:, 2:, 1:-1]
                       + eastward[:, :-2, 1:-1] - 4.0 * zonal_mid)
    merid_laplacian = (northward[:, 1:-1, 2:] + northward[:, 1:-1, :-2] + northward[:, 2:, 1:-1]
                       + northward[:, :-2, 1:-1] - 4.0 * merid_mid)
    press_mid = pressure[:, 1:-1, 1:-1]
    east_star = east_mid * (zonal_mid + time_step * (coriolis * north_avg - (pressure[:, 1:-1, 2:] - press_mid)
                                                      + viscosity * zonal_laplacian))
    north_star = north_mid * (merid_mid + time_step * (-coriolis * east_avg - (pressure[:, 2:, 1:-1] - press_mid)
                                                       + viscosity * merid_laplacian))
    return stars[0], stars[1], east_star, north_star, ocean_mid, east_mid, north_mid


def banded_thomas_elimination(coupling, source):
    layer_number = source.shape[0]
    upper_prime = []
    source_prime = []
    for level_index in range(layer_number):
        divisor = jnp.ones_like(source[level_index])
        numerator = source[level_index]
        if level_index > 0:
            lower_here = -time_step * coupling[level_index - 1]
            divisor = divisor - lower_here - lower_here * upper_prime[level_index - 1]
            numerator = numerator - lower_here * source_prime[level_index - 1]
        if level_index < layer_number - 1:
            upper_here = -time_step * coupling[level_index]
            divisor = divisor - upper_here
            upper_prime.append(upper_here / divisor)
        else:
            upper_prime.append(jnp.zeros_like(numerator))
        source_prime.append(numerator / divisor)
    solved = [None] * layer_number
    solved[layer_number - 1] = source_prime[layer_number - 1]
    for level_index in range(layer_number - 2, -1, -1):
        solved[level_index] = source_prime[level_index] - upper_prime[level_index] * solved[level_index + 1]
    return jnp.stack(solved, axis=0)


def extend_ghost_margin(field, ghost):
    south = jnp.zeros_like(ghost)
    lat_extended = jnp.concatenate([south[..., None, :], field, ghost[..., None, :]], axis=-2)
    return jnp.concatenate([lat_extended[..., -1:], lat_extended, lat_extended[..., :1]], axis=-1)


def reference(heat_anomaly, saltiness_anomaly, zonal_edge_current, meridional_edge_current, interface_mixing_coefficient, ocean_layer_number):
    depth_plain = ocean_layer_number.astype(jnp.float32)
    heat_grid_values = extend_ghost_margin(heat_anomaly, heat_anomaly[:, -1, ::-1])
    salt_field = extend_ghost_margin(saltiness_anomaly, saltiness_anomaly[:, -1, ::-1])
    eastward = extend_ghost_margin(zonal_edge_current, -jnp.roll(zonal_edge_current[:, -1, ::-1], -1, axis=-1))
    northward = extend_ghost_margin(meridional_edge_current, -meridional_edge_current[:, -1, ::-1])
    depth_field = extend_ghost_margin(depth_plain, depth_plain[-1, ::-1])
    row_centres = jnp.arange(MERIDIAN_POINTS).astype(jnp.float32)
    coriolis = (coriolis_coef * (2.0 * (row_centres + 0.5) / MERIDIAN_POINTS - 1.0))[None, :, None]
    heat_interim_guess, salt_star, east_star, north_star, ocean_mid, east_mid, north_mid = tendencies(
        heat_grid_values, salt_field, eastward, northward, depth_field, coriolis)
    scalar_coupling_coefs = interface_mixing_coefficient * ocean_mid[1:]
    heat_next = banded_thomas_elimination(scalar_coupling_coefs, heat_interim_guess)
    saltiness_next = banded_thomas_elimination(scalar_coupling_coefs, salt_star)
    zonal_current_next = banded_thomas_elimination(vertical_viscosity * east_mid[1:], east_star)
    meridional_current_next = banded_thomas_elimination(vertical_viscosity * north_mid[1:], north_star)
    return heat_next, saltiness_next, zonal_current_next, meridional_current_next
```

```python
import jax
import jax.numpy as jnp
from jax import lax
from jax.experimental import pallas as pl
from jax.experimental.pallas import tpu as pltpu
from jax.sharding import PartitionSpec as P

DT = 0.2
CORIOLIS = 1.5
PRESSURE = 0.05
VISC_STEP = 0.1

ROWS, LANES = 8, 128
COL_ROWS = 40


def elimination_constants(levels):
    inner, last = [], []
    for k in range(levels):
        above = VISC_STEP * VISC_STEP * inner[k - 1] if k else 0.0
        step = VISC_STEP if k else 0.0
        inner.append(1.0 / (1.0 + step + VISC_STEP - above))
        last.append(1.0 / (1.0 + step - above))
    return inner, last


def lane_ids():
    return lax.broadcasted_iota(jnp.int32, (ROWS, LANES), 1)


def row_ids():
    return lax.broadcasted_iota(jnp.int32, (ROWS, LANES), 0)


def roll(x, shift, axis):
    return pltpu.roll(x, shift % x.shape[axis], axis)


def density_of(t, s):
    return -(1.0 + 0.1 * t) * t + 0.8 * s - 0.1 * t * s


def level_to_lane(rows, lane):
    k = lax.broadcasted_iota(jnp.int32, rows.shape, 0)
    l = lax.broadcasted_iota(jnp.int32, rows.shape, 1)
    return jnp.sum(jnp.where(k == l, rows[:, lane : lane + 1], 0.0), axis=0, keepdims=True)


def pack_rows(place, levels, t, s, u, v, depth, to_a, to_b, corner):
    even = lax.rem(place[0], 2) == 0
    packed = []
    for f, ref in enumerate((t, s, u, v)):
        top = ref[pl.ds(ROWS - 1, levels, stride=ROWS), :]
        low = ref[pl.ds(0, levels, stride=ROWS), :]
        to_a[pl.ds(f, levels, stride=4), :] = jnp.where(even, top, low)
        b = jnp.where(even, low, top)
        to_b[pl.ds(f, levels, stride=4), :] = b
        packed.append(b)
    h = depth[...].astype(jnp.float32)
    blank = jnp.zeros((3, LANES), jnp.float32)
    last = 4 * levels
    to_a[last : last + 4, :] = jnp.concatenate([jnp.where(even, h[7:8], h[0:1]), blank], axis=0)
    to_b[last : last + 4, :] = jnp.concatenate([jnp.where(even, h[0:1], h[7:8]), blank], axis=0)
    cu = level_to_lane(packed[2], LANES - 1)
    cv = level_to_lane(packed[3], 0)
    row = row_ids()
    corner[...] = jnp.where(row == 0, cu, jnp.where(row == 1, cv, 0.0))


def pack_columns(place, levels, t, s, u, v, depth, from_a, to_c, to_d):
    lat_even = lax.rem(place[0], 2) == 0
    lon_even = lax.rem(place[1], 2) == 0
    lane = lane_ids()
    h = depth[...].astype(jnp.float32)
    for f, ref in enumerate((t, s, u, v)):
        east = jnp.zeros((ROWS, LANES), jnp.float32)
        west = jnp.zeros((ROWS, LANES), jnp.float32)
        for k in range(levels):
            x = ref[k * ROWS : (k + 1) * ROWS, :]
            east = jnp.where(lane == k, x[:, LANES - 1 : LANES], east)
            west = jnp.where(lane == k, x[:, 0:1], west)
        if f == 0:
            east = jnp.where(lane == levels, h[:, LANES - 1 : LANES], east)
            west = jnp.where(lane == levels, h[:, 0:1], west)
        to_c[f * ROWS : (f + 1) * ROWS, :] = jnp.where(lon_even, east, west)
        to_d[f * ROWS : (f + 1) * ROWS, :] = jnp.where(lon_even, west, east)
    cu = level_to_lane(from_a[pl.ds(2, levels, stride=4), :], LANES - 1)
    cv = level_to_lane(from_a[pl.ds(3, levels, stride=4), :], 0)
    east = jnp.broadcast_to(jnp.where(lat_even, cu, 0.0), (ROWS, LANES))
    west = jnp.broadcast_to(jnp.where(lat_even, 0.0, cv), (ROWS, LANES))
    to_c[4 * ROWS : 5 * ROWS, :] = jnp.where(lon_even, east, west)
    to_d[4 * ROWS : 5 * ROWS, :] = jnp.where(lon_even, west, east)


def coriolis_rows(place, total):
    row = (place[0] * ROWS + row_ids()).astype(jnp.float32)
    return CORIOLIS * (2.0 * (row + 0.5) / total - 1.0)


def local_work(place, levels, total, t, s, u, v, mix, depth, st, ss, su, sv, ra, aa, ba):
    lane, row = lane_ids(), row_ids()
    h = depth[...].astype(jnp.float32)
    f4 = (0.25 * DT) * coriolis_rows(place, total)
    not_e, not_w = lane < LANES - 1, lane > 0
    not_n, not_s = row < ROWS - 1, row > 0
    open_e = jnp.where(not_e, jnp.minimum(h, roll(h, -1, 1)), 0.0)
    open_n = jnp.where(not_n, jnp.minimum(h, roll(h, -1, 0)), 0.0)
    summed = jnp.zeros((ROWS, LANES), jnp.float32)
    b_prev = jnp.zeros((ROWS, LANES), jnp.float32)
    c_here = jnp.zeros((ROWS, LANES), jnp.float32)
    zero = jnp.zeros((ROWS, LANES), jnp.float32)
    for k in range(levels):
        tk, sk, uk, vk = t[k], s[k], u[k], v[k]
        wet = h > float(k)
        dens = jnp.where(wet, density_of(tk, sk), 0.0)
        summed = summed + dens
        p = PRESSURE * (summed - 0.5 * dens)
        me, mn = open_e > float(k), open_n > float(k)
        half_u, half_v = 0.5 * uk, 0.5 * vk
        for x, out in ((tk, st), (sk, ss)):
            xe, xn = roll(x, -1, 1), roll(x, -1, 0)
            fe = jnp.where(me, half_u * (x + xe) - 0.5 * (xe - x), 0.0)
            fn = jnp.where(mn, half_v * (x + xn) - 0.5 * (xn - x), 0.0)
            out[k] = x - DT * (fe - roll(fe, 1, 1) + fn - roll(fn, 1, 0))
        ue = jnp.where(not_e, roll(uk, -1, 1), 0.0)
        uw = jnp.where(not_w, roll(uk, 1, 1), 0.0)
        un = jnp.where(not_n, roll(uk, -1, 0), 0.0)
        us = jnp.where(not_s, roll(uk, 1, 0), 0.0)
        unw = jnp.where(not_n, roll(uw, -1, 0), 0.0)
        ve = jnp.where(not_e, roll(vk, -1, 1), 0.0)
        vw = jnp.where(not_w, roll(vk, 1, 1), 0.0)
        vn = jnp.where(not_n, roll(vk, -1, 0), 0.0)
        vs = jnp.where(not_s, roll(vk, 1, 0), 0.0)
        vse = jnp.where(not_s, roll(ve, 1, 0), 0.0)
        pe = jnp.where(not_e, roll(p, -1, 1), 0.0)
        pn = jnp.where(not_n, roll(p, -1, 0), 0.0)
        su[k] = (
            uk + f4 * (vk + ve + vs + vse) - DT * (pe - p) + 0.1 * (ue + uw + un + us - 4.0 * uk)
        )
        sv[k] = (
            vk - f4 * (uk + uw + un + unw) - DT * (pn - p) + 0.1 * (ve + vw + vn + vs - 4.0 * vk)
        )
        c_next = jnp.where(h > float(k + 1), DT * mix[k], 0.0) if k < levels - 1 else zero
        r = 1.0 / (1.0 + c_here + c_next - c_here * b_prev)
        r = jnp.where(wet, r, 0.0)
        ra[k] = r
        aa[k] = c_here * r
        b_prev = c_next * r
        ba[k] = b_prev
        c_here = c_next


def finish(
    place, levels, total, st, ss, su, sv, ra, aa, ba, depth,
    to_a, to_b, from_a, from_b, to_c, to_d, from_c, from_d, corner,
    ot, os, ou, ov, north, south, east, west, kept,
):
    lane, row = lane_ids(), row_ids()
    lat_even = lax.rem(place[0], 2) == 0
    lon_even = lax.rem(place[1], 2) == 0
    top = place[2] == 1
    h = depth[...].astype(jnp.float32)
    f4 = (0.25 * DT) * coriolis_rows(place, total)
    f7, f0 = f4[7:8, :], f4[0:1, :]

    kk = lax.broadcasted_iota(jnp.int32, (levels, LANES), 0).astype(jnp.float32)
    ll = lax.broadcasted_iota(jnp.int32, (levels, LANES), 1)

    def north_of(f):
        return jnp.where(
            lat_even, from_a[pl.ds(f, levels, stride=4), :], from_b[pl.ds(f, levels, stride=4), :]
        )

    def south_of(f):
        return jnp.where(
            lat_even, from_b[pl.ds(f, levels, stride=4), :], from_a[pl.ds(f, levels, stride=4), :]
        )

    def row_7(f):
        return jnp.where(
            lat_even, to_a[pl.ds(f, levels, stride=4), :], to_b[pl.ds(f, levels, stride=4), :]
        )

    def row_0(f):
        return jnp.where(
            lat_even, to_b[pl.ds(f, levels, stride=4), :], to_a[pl.ds(f, levels, stride=4), :]
        )

    def mirrored(x, last):
        ids = lax.rem(last + LANES - lax.broadcasted_iota(jnp.int32, x.shape, 1), LANES)
        return jnp.take_along_axis(x, ids, axis=1)

    at = 4 * levels
    h_a, h_b = from_a[at : at + 1, :], from_b[at : at + 1, :]
    h_n = jnp.where(lat_even, h_a, h_b)
    h_s = jnp.where(lat_even, h_b, h_a)
    h_n8 = jnp.broadcast_to(h_n, (ROWS, LANES))
    h_n8 = jnp.where(top, mirrored(h_n8, LANES - 1), h_n8)
    h_n = h_n8[0:1, :]
    tn, sn, un, vn = (north_of(f) for f in range(4))
    tn = jnp.where(top, mirrored(tn, LANES - 1), tn)
    sn = jnp.where(top, mirrored(sn, LANES - 1), sn)
    vn = jnp.where(top, -mirrored(vn, LANES - 1), vn)
    un = jnp.where(top, -mirrored(un, LANES - 2), un)
    unw = roll(un, 1, 1)
    unw = jnp.where(jnp.logical_or(top, ll > 0), unw, 0.0)
    un = jnp.where(jnp.logical_and(top, ll == LANES - 1), 0.0, un)
    t7, s7, v7 = row_7(0), row_7(1), row_7(3)
    mask = jnp.minimum(h[7:8, :], h_n) > kk
    north[0, :levels, :] = jnp.where(mask, -0.1 * (v7 * (t7 + tn) - (tn - t7)), 0.0)
    north[1, :levels, :] = jnp.where(mask, -0.1 * (v7 * (s7 + sn) - (sn - s7)), 0.0)
    north[2, :levels, :] = 0.1 * un
    north[3, :levels, :] = 0.1 * vn - f7 * (un + unw)
    north[4, :levels, :] = jnp.where(h_n > kk, (DT * PRESSURE) * density_of(tn, sn), 0.0)

    ts, ssouth, us, vs = (south_of(f) for f in range(4))
    t0, s0 = row_0(0), row_0(1)
    mask = jnp.minimum(h[0:1, :], h_s) > kk
    south[0, :levels, :] = jnp.where(mask, 0.1 * (vs * (ts + t0) - (t0 - ts)), 0.0)
    south[1, :levels, :] = jnp.where(mask, 0.1 * (vs * (ssouth + s0) - (s0 - ssouth)), 0.0)
    vse = jnp.where(ll < LANES - 1, roll(vs, -1, 1), 0.0)
    south[2, :levels, :] = 0.1 * us + f0 * (vs + vse)
    south[3, :levels, :] = 0.1 * vs

    def tile(even_ref, odd_ref, f):
        at = slice(f * ROWS, (f + 1) * ROWS)
        return jnp.where(lon_even, even_ref[at, :], odd_ref[at, :])

    kl = lane.astype(jnp.float32)
    te, se, ue, ve, ce = (tile(from_c, from_d, f) for f in range(5))
    tw, sw, uw, vw, cw = (tile(from_d, from_c, f) for f in range(5))
    t127, s127, u127 = (tile(to_c, to_d, f) for f in range(3))
    tz, sz = (tile(to_d, to_c, f) for f in range(2))
    cb_u = jnp.broadcast_to(corner[0:1, :], (ROWS, LANES))
    cb_v = jnp.broadcast_to(corner[1:2, :], (ROWS, LANES))
    south_east = jnp.where(lat_even, cb_v, ce)
    north_west = jnp.where(lat_even, cw, jnp.where(top, 0.0, cb_u))
    north_end = jnp.where(top, -cb_u, 0.0)
    h_e = te[:, levels : levels + 1]
    h_w = tw[:, levels : levels + 1]
    mask = jnp.minimum(h[:, LANES - 1 : LANES], h_e) > kl
    dt_e = jnp.where(mask, -0.1 * (u127 * (t127 + te) - (te - t127)), 0.0)
    ds_e = jnp.where(mask, -0.1 * (u127 * (s127 + se) - (se - s127)), 0.0)
    mask = jnp.minimum(h[:, 0:1], h_w) > kl
    dt_w = jnp.where(mask, 0.1 * (uw * (tw + tz) - (tz - tw)), 0.0)
    ds_w = jnp.where(mask, 0.1 * (uw * (sw + sz) - (sz - sw)), 0.0)
    dens = jnp.where(h_e > kl, density_of(te, se), 0.0)
    summed = dens
    for step in (1, 2, 4, 8, 16, 32, 64):
        summed = summed + jnp.where(lane >= step, roll(summed, step, 1), 0.0)
    pe = PRESSURE * (summed - 0.5 * dens)
    ve_up = jnp.where(row > 0, roll(ve, 1, 0), south_east)
    uw_dn = jnp.where(row < ROWS - 1, roll(uw, -1, 0), north_west)
    end = jnp.where(row == ROWS - 1, north_end, 0.0)
    du_e = f4 * (ve + ve_up) - DT * pe + 0.1 * ue + 0.1 * end
    du_w = 0.1 * uw
    dv_e = 0.1 * ve - f4 * end
    dv_w = 0.1 * vw - f4 * (uw + uw_dn)

    m_u = jnp.minimum(h, jnp.where(lane < LANES - 1, roll(h, -1, 1), h_e))
    m_v = jnp.minimum(h, jnp.where(row < ROWS - 1, roll(h, -1, 0), h_n))
    at_n, at_s = row == ROWS - 1, row == 0
    at_e, at_w = lane == LANES - 1, lane == 0
    inner, last = elimination_constants(levels)
    pt = ps = pu = pv = jnp.zeros((ROWS, LANES), jnp.float32)
    cs = jnp.zeros((1, LANES), jnp.float32)
    for k in range(levels):
        def spread(f, de, dw, extra=None):
            n = north[f, k : k + 1, :]
            if extra is not None:
                n = n - extra
            base = jnp.where(at_n, n, jnp.where(at_s, south[f, k : k + 1, :], 0.0))
            side = jnp.where(at_e, de[:, k : k + 1], jnp.where(at_w, dw[:, k : k + 1], 0.0))
            return base + side

        dn = north[4, k : k + 1, :]
        cs = cs + dn
        r, a = ra[k], aa[k]
        pt = r * (st[k] + spread(0, dt_e, dt_w)) + a * pt
        ps = r * (ss[k] + spread(1, ds_e, ds_w)) + a * ps
        ru = jnp.where(m_u > float(k + 1), inner[k], jnp.where(m_u > float(k), last[k], 0.0))
        rv = jnp.where(m_v > float(k + 1), inner[k], jnp.where(m_v > float(k), last[k], 0.0))
        pu = ru * (su[k] + spread(2, du_e, du_w)) + (VISC_STEP * ru) * pu
        pv = rv * (sv[k] + spread(3, dv_e, dv_w, cs - 0.5 * dn)) + (VISC_STEP * rv) * pv
        kept[0, k] = pt
        kept[1, k] = ps
        kept[2, k] = pu
        kept[3, k] = pv
    xt, xs, xu, xv = pt, ps, pu, pv
    for k in range(levels - 1, -1, -1):
        if k < levels - 1:
            b = ba[k]
            bu = jnp.where(m_u > float(k + 1), VISC_STEP * inner[k], 0.0)
            bv = jnp.where(m_v > float(k + 1), VISC_STEP * inner[k], 0.0)
            xt = kept[0, k] + b * xt
            xs = kept[1, k] + b * xs
            xu = kept[2, k] + bu * xu
            xv = kept[3, k] + bv * xv
        ot[k] = xt
        os[k] = xs
        ou[k] = xu
        ov[k] = xv


SMEM = pl.BlockSpec(memory_space=pltpu.SMEM)
VMEM = pl.BlockSpec(memory_space=pltpu.VMEM)


def call(body, outs, n_in, scratch=(), name=None):
    return pl.pallas_call(
        body,
        out_shape=tuple(jax.ShapeDtypeStruct(s, jnp.float32) for s in outs),
        in_specs=[SMEM] + [VMEM] * n_in,
        out_specs=tuple(VMEM for _ in outs),
        scratch_shapes=list(scratch),
        name=name,
    )


def exchanges(n_lat, n_lon):
    def at(lat, lon):
        return (lon % n_lon) * n_lat + lat

    def both(x, y):
        return [(x, y), (y, x)]

    a, b, corner, c, d = [], [], [], [], []
    for lon in range(n_lon):
        for lat in range(0, n_lat, 2):
            a += both(at(lat, lon), at(lat + 1, lon))
        for lat in range(1, n_lat - 1, 2):
            b += both(at(lat, lon), at(lat + 1, lon))
            corner += both(at(lat, lon), at(lat + 1, lon - 1))
        b.append((at(n_lat - 1, lon), at(n_lat - 1, n_lon - 1 - lon)))
        corner.append((at(n_lat - 1, lon), at(n_lat - 1, n_lon - 2 - lon)))
    for lat in range(n_lat):
        for lon in range(0, n_lon, 2):
            c += both(at(lat, lon), at(lat, lon + 1))
            d += both(at(lat, lon + 1), at(lat, lon + 2))
    return a, b, corner, c, d


def local(t, s, u, v, mix, depth):
    levels = t.shape[0]
    n_lat, n_lon = lax.axis_size("lat"), lax.axis_size("lon")
    total = float(n_lat * ROWS)
    lat, lon = lax.axis_index("lat"), lax.axis_index("lon")
    place = jnp.stack([lat, lon, (lat == n_lat - 1).astype(jnp.int32)]).astype(jnp.int32)
    pairs_a, pairs_b, pairs_corner, pairs_c, pairs_d = exchanges(n_lat, n_lon)
    axes = ("lon", "lat")
    flat = [x.reshape(levels * ROWS, LANES) for x in (t, s, u, v)]
    row_shape = (4 * levels + 4, LANES)
    full = (levels, ROWS, LANES)

    to_a, to_b, to_corner = call(
        lambda place, *refs: pack_rows(place, levels, *refs),
        [row_shape, row_shape, (ROWS, LANES)], 5, name="pack_rows",
    )(place, *flat, depth)
    from_b = lax.ppermute(to_b, axes, pairs_b)
    corner = lax.ppermute(to_corner, axes, pairs_corner)
    from_a = lax.ppermute(to_a, axes, pairs_a)
    to_c, to_d = call(
        lambda place, *refs: pack_columns(place, levels, *refs),
        [(COL_ROWS, LANES)] * 2, 6, name="pack_columns",
    )(place, *flat, depth, from_a)
    from_d = lax.ppermute(to_d, axes, pairs_d)
    from_c = lax.ppermute(to_c, axes, pairs_c)
    work = call(
        lambda place, *refs: local_work(place, levels, total, *refs), [full] * 7, 6, name="local_work"
    )(place, t, s, u, v, mix, depth)
    padded = (levels + 7) // 8 * 8
    return call(
        lambda place, *refs: finish(place, levels, total, *refs),
        [full] * 4,
        17,
        [
            pltpu.VMEM((5, padded, LANES), jnp.float32),
            pltpu.VMEM((4, padded, LANES), jnp.float32),
            pltpu.VMEM((4, ROWS, LANES), jnp.float32),
            pltpu.VMEM((4, ROWS, LANES), jnp.float32),
            pltpu.VMEM((4,) + full, jnp.float32),
        ],
        name="finish",
    )(place, *work, depth, to_a, to_b, from_a, from_b, to_c, to_d, from_c, from_d, corner)


def solution(mesh):
    field = P(None, "lat", "lon")
    return jax.shard_map(
        local,
        mesh=mesh,
        in_specs=(field,) * 5 + (P("lat", "lon"),),
        out_specs=(field,) * 4,
        check_vma=False,
    )
```

```python
import jax
import jax.numpy as jnp
from jax import lax
from jax.experimental import pallas as pl
from jax.experimental.pallas import tpu as pltpu
from jax.sharding import PartitionSpec as P


DT = 0.2
CORIOLIS = 1.5
PRESSURE = 0.05
VISC_STEP = 0.1

ROWS, LANES = 8, 128
VMEM_GRANT = 8 << 20
COL_ROWS = 40


def elimination_constants(levels):
    inner, last = [], []
    for k in range(levels):
        above = VISC_STEP * VISC_STEP * inner[k - 1] if k else 0.0
        step = VISC_STEP if k else 0.0
        inner.append(1.0 / (1.0 + step + VISC_STEP - above))
        last.append(1.0 / (1.0 + step - above))
    return inner, last


def lane_ids():
    return lax.broadcasted_iota(jnp.int32, (ROWS, LANES), 1)


def row_ids():
    return lax.broadcasted_iota(jnp.int32, (ROWS, LANES), 0)


def roll(x, shift, axis):
    return pltpu.roll(x, shift % x.shape[axis], axis)


def density_of(t, s):
    return -(1.0 + 0.1 * t) * t + 0.8 * s - 0.1 * t * s


def level_to_lane(rows, lane):
    k = lax.broadcasted_iota(jnp.int32, rows.shape, 0)
    l = lax.broadcasted_iota(jnp.int32, rows.shape, 1)
    return jnp.sum(jnp.where(k == l, rows[:, lane : lane + 1], 0.0), axis=0, keepdims=True)


def place_of(n_lat, n_lon):
    lat, lon = lax.axis_index("lat"), lax.axis_index("lon")
    return lat, lon, lax.rem(lat, 4) < 2, lat == n_lat - 1, lon == n_lon - 1


def pack_rows(mesh_size, levels, t, s, u, v, depth, t_out, s_out, u_out, v_out, h_out, to_a, to_b, corner, ints, sems):
    lat, _, _, _, _ = place_of(*mesh_size)
    even = lax.rem(lat, 2) == 0
    outs = (t_out, s_out, u_out, v_out)
    copies = [
        pltpu.make_async_copy(x, y, sems.at[f]) for f, (x, y) in enumerate(zip((t, s, u, v), outs))
    ]
    copies.append(pltpu.make_async_copy(depth, ints, sems.at[4]))
    for copy in copies:
        copy.start()
    copies[4].wait()
    h = ints[...].astype(jnp.float32)
    h_out[...] = h
    blank = jnp.zeros((3, LANES), jnp.float32)
    last = 4 * levels
    to_a[last : last + 4, :] = jnp.concatenate([jnp.where(even, h[7:8], h[0:1]), blank], axis=0)
    to_b[last : last + 4, :] = jnp.concatenate([jnp.where(even, h[0:1], h[7:8]), blank], axis=0)
    packed = []
    for f, ref in enumerate(outs):
        copies[f].wait()
        top = ref[pl.ds(ROWS - 1, levels, stride=ROWS), :]
        low = ref[pl.ds(0, levels, stride=ROWS), :]
        to_a[pl.ds(f, levels, stride=4), :] = jnp.where(even, top, low)
        b = jnp.where(even, low, top)
        to_b[pl.ds(f, levels, stride=4), :] = b
        packed.append(b)
    cu = level_to_lane(packed[2], LANES - 1)
    cv = level_to_lane(packed[3], 0)
    row = row_ids()
    corner[...] = jnp.where(row == 0, cu, jnp.where(row == 1, cv, 0.0))


def pack_columns(mesh_size, levels, early, t, s, u, v, depth, from_a, *refs):
    to_c, to_d = refs[-2:]
    lat, lon, first, _, _ = place_of(*mesh_size)
    lat_even = lax.rem(lat, 2) == 0
    lon_even = lax.rem(lon, 2) == 0
    if not early:

        @pl.when(first)
        def _():
            to_c[...] = refs[0][...]
            to_d[...] = refs[1][...]

    @pl.when(first if early else jnp.logical_not(first))
    def _():
        lane = lane_ids()
        h = depth[...]
        for f, ref in enumerate((t, s, u, v)):
            east = jnp.zeros((ROWS, LANES), jnp.float32)
            west = jnp.zeros((ROWS, LANES), jnp.float32)
            for k in range(levels):
                x = ref[k * ROWS : (k + 1) * ROWS, :]
                east = jnp.where(lane == k, x[:, LANES - 1 : LANES], east)
                west = jnp.where(lane == k, x[:, 0:1], west)
            if f == 0:
                east = jnp.where(lane == levels, h[:, LANES - 1 : LANES], east)
                west = jnp.where(lane == levels, h[:, 0:1], west)
            to_c[f * ROWS : (f + 1) * ROWS, :] = jnp.where(lon_even, east, west)
            to_d[f * ROWS : (f + 1) * ROWS, :] = jnp.where(lon_even, west, east)
        cu = level_to_lane(from_a[pl.ds(2, levels, stride=4), :], LANES - 1)
        cv = level_to_lane(from_a[pl.ds(3, levels, stride=4), :], 0)
        east = jnp.broadcast_to(jnp.where(lat_even, cu, 0.0), (ROWS, LANES))
        west = jnp.broadcast_to(jnp.where(lat_even, 0.0, cv), (ROWS, LANES))
        to_c[4 * ROWS : 5 * ROWS, :] = jnp.where(lon_even, east, west)
        to_d[4 * ROWS : 5 * ROWS, :] = jnp.where(lon_even, west, east)


def coriolis_rows(lat, total):
    row = (lat * ROWS + row_ids()).astype(jnp.float32)
    return CORIOLIS * (2.0 * (row + 0.5) / total - 1.0)


def local_work(mesh_size, levels, total, early, *refs):
    t, s, u, v, mix, depth = refs[:6]
    st, ss, su, sv, ra, aa, ba = refs[-7:]
    lat, _, first, _, _ = place_of(*mesh_size)

    @pl.when(first if early else jnp.logical_not(first))
    def _():
        lane, row = lane_ids(), row_ids()
        h = depth[...]
        f4 = (0.25 * DT) * coriolis_rows(lat, total)
        open_e = jnp.where(lane < LANES - 1, jnp.minimum(h, roll(h, -1, 1)), 0.0)
        open_n = jnp.where(row < ROWS - 1, jnp.minimum(h, roll(h, -1, 0)), 0.0)
        zero = jnp.zeros((ROWS, LANES), jnp.float32)
        one = jnp.ones((ROWS, LANES), jnp.float32)
        summed, c_here = zero, zero
        minor, minor_prev = one, zero
        for k in range(levels):
            at = slice(k * ROWS, (k + 1) * ROWS)
            tk, sk, uk, vk = t[at, :], s[at, :], u[at, :], v[at, :]
            wet = h > float(k)
            dens = jnp.where(wet, PRESSURE * density_of(tk, sk), 0.0)
            summed = summed + dens
            p = summed - 0.5 * dens
            me, mn = open_e > float(k), open_n > float(k)
            half_u, half_v = 0.5 * uk, 0.5 * vk
            e0, e1 = jnp.where(me, half_u + 0.5, 0.0), jnp.where(me, half_u - 0.5, 0.0)
            n0, n1 = jnp.where(mn, half_v + 0.5, 0.0), jnp.where(mn, half_v - 0.5, 0.0)
            for x, out in ((tk, st), (sk, ss)):
                fe = e0 * x + e1 * roll(x, -1, 1)
                fn = n0 * x + n1 * roll(x, -1, 0)
                out[k] = x - DT * (fe - roll(fe, 1, 1) + fn - roll(fn, 1, 0))
            uw, ve = roll(uk, 1, 1), roll(vk, -1, 1)
            un, vs = roll(uk, -1, 0), roll(vk, 1, 0)
            lap_u = (roll(uk, -1, 1) + uw) + (un + roll(uk, 1, 0)) - 4.0 * uk
            lap_v = (ve + roll(vk, 1, 1)) + (roll(vk, -1, 0) + vs) - 4.0 * vk
            v4 = (vk + ve) + (vs + roll(ve, 1, 0))
            u4 = (uk + uw) + (un + roll(uw, -1, 0))
            su[k] = uk + f4 * v4 - DT * (roll(p, -1, 1) - p) + 0.1 * lap_u
            sv[k] = vk - f4 * u4 - DT * (roll(p, -1, 0) - p) + 0.1 * lap_v
            c_next = jnp.where(h > float(k + 1), DT * mix[k], 0.0) if k < levels - 1 else zero
            minor_next = (1.0 + c_here + c_next) * minor - (c_here * c_here) * minor_prev
            r = jnp.where(wet, minor / minor_next, 0.0)
            minor_prev, minor = minor, minor_next
            ra[k] = r
            aa[k] = c_here * r
            ba[k] = c_next * r
            c_here = c_next


def finish(mesh_size, levels, total, *refs):
    (st, ss, su, sv, ra, aa, ba, depth, to_a, to_b, a_p, a_q, b_p, b_q, c_own, d_own,
     c_p, d_p, c_q, d_q, corner_p, corner_q, ot, os, ou, ov, north, south, kept) = refs
    lat, lon, first, top, lon_last = place_of(*mesh_size)
    lane, row = lane_ids(), row_ids()
    lat_even = lax.rem(lat, 2) == 0
    lon_even = lax.rem(lon, 2) == 0
    b_first = jnp.logical_or(first, top)
    d_first = jnp.logical_and(first, jnp.logical_not(lon_last))
    h = depth[...]
    f4 = (0.25 * DT) * coriolis_rows(lat, total)
    f7, f0 = f4[7:8, :], f4[0:1, :]

    kk = lax.broadcasted_iota(jnp.int32, (levels, LANES), 0).astype(jnp.float32)
    ll = lax.broadcasted_iota(jnp.int32, (levels, LANES), 1)

    def field(ref, f):
        return ref[pl.ds(f, levels, stride=4), :]

    def ghosts(f):
        a = jnp.where(first, field(a_p, f), field(a_q, f))
        b = jnp.where(b_first, field(b_p, f), field(b_q, f))
        return jnp.where(lat_even, a, b), jnp.where(lat_even, b, a)

    def own(f):
        a, b = field(to_a, f), field(to_b, f)
        return jnp.where(lat_even, a, b), jnp.where(lat_even, b, a)

    def mirrored(x, last):
        ids = lax.rem(last + LANES - lax.broadcasted_iota(jnp.int32, x.shape, 1), LANES)
        return jnp.take_along_axis(x, ids, axis=1)

    at = slice(4 * levels, 4 * levels + 1)
    h_a = jnp.where(first, a_p[at, :], a_q[at, :])
    h_b = jnp.where(b_first, b_p[at, :], b_q[at, :])
    h_n = jnp.broadcast_to(jnp.where(lat_even, h_a, h_b), (ROWS, LANES))
    h_n = jnp.where(top, mirrored(h_n, LANES - 1), h_n)[0:1, :]
    h_s = jnp.where(lat_even, h_b, h_a)
    (tn, ts), (sn, ss_), (un, us), (vn, vs) = (ghosts(f) for f in range(4))
    (t7, t0), (s7, s0), (u7, u0), (v7, v0) = (own(f) for f in range(4))
    tn = jnp.where(top, mirrored(tn, LANES - 1), tn)
    sn = jnp.where(top, mirrored(sn, LANES - 1), sn)
    vn = jnp.where(top, -mirrored(vn, LANES - 1), vn)
    un = jnp.where(top, -mirrored(un, LANES - 2), un)
    unw = roll(un, 1, 1)
    unw = jnp.where(ll > 0, unw - roll(u0, 1, 1), jnp.where(top, unw, 0.0))
    un = jnp.where(jnp.logical_and(top, ll == LANES - 1), 0.0, un) - u0
    mask = jnp.minimum(h[7:8, :], h_n) > kk
    north[0, :levels, :] = jnp.where(mask, -0.1 * (v7 * (t7 + tn) - (tn - t7)), 0.0)
    north[1, :levels, :] = jnp.where(mask, -0.1 * (v7 * (s7 + sn) - (sn - s7)), 0.0)
    north[2, :levels, :] = 0.1 * un
    north[3, :levels, :] = 0.1 * (vn - v0) - f7 * (un + unw)
    north[4, :levels, :] = (DT * PRESSURE) * (
        jnp.where(h_n > kk, density_of(tn, sn), 0.0)
        - jnp.where(h[0:1, :] > kk, density_of(t0, s0), 0.0)
    )
    mask = jnp.minimum(h[0:1, :], h_s) > kk
    south[0, :levels, :] = jnp.where(mask, 0.1 * (vs * (ts + t0) - (t0 - ts)), 0.0)
    south[1, :levels, :] = jnp.where(mask, 0.1 * (vs * (ss_ + s0) - (s0 - ss_)), 0.0)
    vs = vs - v7
    vse = jnp.where(ll < LANES - 1, roll(vs, -1, 1), 0.0)
    south[2, :levels, :] = 0.1 * (us - u7) + f0 * (vs + vse)
    south[3, :levels, :] = 0.1 * vs

    kl = lane.astype(jnp.float32)

    def tiles(c, d, f):
        at = slice(f * ROWS, (f + 1) * ROWS)
        x = jnp.where(first, c[0][at, :], c[1][at, :])
        y = jnp.where(d[2], d[0][at, :], d[1][at, :])
        return jnp.where(lon_even, x, y), jnp.where(lon_even, y, x)

    got_c, got_d = (c_p, c_q), (d_p, d_q, d_first)
    own_c, own_d = (c_own, c_own), (d_own, d_own, first)
    (te, tw), (se, sw), (ue, uw), (ve, vw), (ce, cw) = (tiles(got_c, got_d, f) for f in range(5))
    (t9, tz), (s9, sz), (u9, uz), (v9, vz) = (tiles(own_c, own_d, f) for f in range(4))
    cb = jnp.where(b_first, corner_p[...], corner_q[...])
    cb_u = jnp.broadcast_to(cb[0:1, :], (ROWS, LANES))
    cb_v = jnp.broadcast_to(cb[1:2, :], (ROWS, LANES))
    south_east = jnp.where(lat_even, cb_v, ce)
    north_west = jnp.where(lat_even, cw, jnp.where(top, 0.0, cb_u))
    north_end = jnp.where(jnp.logical_and(top, row == ROWS - 1), -cb_u, 0.0)
    h_e = te[:, levels : levels + 1]
    h_w = tw[:, levels : levels + 1]
    mask = jnp.minimum(h[:, LANES - 1 : LANES], h_e) > kl
    dt_e = jnp.where(mask, -0.1 * (u9 * (t9 + te) - (te - t9)), 0.0)
    ds_e = jnp.where(mask, -0.1 * (u9 * (s9 + se) - (se - s9)), 0.0)
    mask = jnp.minimum(h[:, 0:1], h_w) > kl
    dt_w = jnp.where(mask, 0.1 * (uw * (tw + tz) - (tz - tw)), 0.0)
    ds_w = jnp.where(mask, 0.1 * (uw * (sw + sz) - (sz - sw)), 0.0)
    dens = jnp.where(h_e > kl, density_of(te, se), 0.0) - jnp.where(
        h[:, 0:1] > kl, density_of(tz, sz), 0.0
    )
    summed = dens
    for step in (1, 2, 4, 8, 16, 32, 64):
        summed = summed + jnp.where(lane >= step, roll(summed, step, 1), 0.0)
    pe = (DT * PRESSURE) * (summed - 0.5 * dens)
    ve_up = jnp.where(row > 0, roll(ve, 1, 0), south_east) - roll(vz, 1, 0)
    uw_dn = jnp.where(row < ROWS - 1, roll(uw, -1, 0), north_west) - roll(u9, -1, 0)
    du_e = f4 * ((ve - vz) + ve_up) - pe + 0.1 * (ue - uz) + 0.1 * north_end
    du_w = 0.1 * (uw - u9)
    dv_e = 0.1 * (ve - vz) - f4 * north_end
    dv_w = 0.1 * (vw - v9) - f4 * ((uw - u9) + uw_dn)

    m_u = jnp.minimum(h, jnp.where(lane < LANES - 1, roll(h, -1, 1), h_e))
    m_v = jnp.minimum(h, jnp.where(row < ROWS - 1, roll(h, -1, 0), h_n))
    at_n, at_s = row == ROWS - 1, row == 0
    at_e, at_w = lane == LANES - 1, lane == 0
    inner, last = elimination_constants(levels)
    pt = ps = pu = pv = jnp.zeros((ROWS, LANES), jnp.float32)
    cs = jnp.zeros((1, LANES), jnp.float32)
    for k in range(levels):

        def spread(f, de, dw, extra=None):
            n = north[f, k : k + 1, :]
            if extra is not None:
                n = n - extra
            base = jnp.where(at_n, n, jnp.where(at_s, south[f, k : k + 1, :], 0.0))
            side = jnp.where(at_e, de[:, k : k + 1], jnp.where(at_w, dw[:, k : k + 1], 0.0))
            return base + side

        dn = north[4, k : k + 1, :]
        cs = cs + dn
        r, a = ra[k], aa[k]
        pt = r * (st[k] + spread(0, dt_e, dt_w)) + a * pt
        ps = r * (ss[k] + spread(1, ds_e, ds_w)) + a * ps
        ru = jnp.where(m_u > float(k + 1), inner[k], jnp.where(m_u > float(k), last[k], 0.0))
        rv = jnp.where(m_v > float(k + 1), inner[k], jnp.where(m_v > float(k), last[k], 0.0))
        pu = ru * (su[k] + spread(2, du_e, du_w)) + (VISC_STEP * ru) * pu
        pv = rv * (sv[k] + spread(3, dv_e, dv_w, cs - 0.5 * dn)) + (VISC_STEP * rv) * pv
        kept[0, k] = pt
        kept[1, k] = ps
        kept[2, k] = pu
        kept[3, k] = pv
    xt, xs, xu, xv = pt, ps, pu, pv
    for k in range(levels - 1, -1, -1):
        if k < levels - 1:
            b = ba[k]
            bu = jnp.where(m_u > float(k + 1), VISC_STEP * inner[k], 0.0)
            bv = jnp.where(m_v > float(k + 1), VISC_STEP * inner[k], 0.0)
            xt = kept[0, k] + b * xt
            xs = kept[1, k] + b * xs
            xu = kept[2, k] + bu * xu
            xv = kept[3, k] + bv * xv
        ot[k] = xt
        os[k] = xs
        ou[k] = xu
        ov[k] = xv


HBM = pl.BlockSpec(memory_space=pltpu.HBM)
VMEM = pl.BlockSpec(memory_space=pltpu.VMEM)


def call(body, far, near, outs, scratch=(), aliases=None, keep=True):
    far = [pltpu.with_memory_space_constraint(x, pltpu.HBM) for x in far]
    near = [pltpu.with_memory_space_constraint(x, pltpu.VMEM) for x in near]
    shapes = tuple(
        pltpu.VMEM(s, jnp.float32) if keep else jax.ShapeDtypeStruct(s, jnp.float32) for s in outs
    )
    return pl.pallas_call(
        body,
        out_shape=shapes,
        in_specs=[HBM] * len(far) + [VMEM] * len(near),
        out_specs=tuple(VMEM for _ in outs),
        scratch_shapes=list(scratch),
        input_output_aliases=aliases or {},
        compiler_params=pltpu.CompilerParams(vmem_limit_bytes=VMEM_GRANT),
    )(*far, *near)


def exchanges(n_lat, n_lon):
    def at(lat, lon):
        return (lon % n_lon) * n_lat + lat

    def both(x, y):
        return [(x, y), (y, x)]

    p = {name: [] for name in [x + y for x in "abkcd" for y in ("_p", "_q")]}
    for lon in range(n_lon):
        for lat in range(0, n_lat, 2):
            p["a_p" if lat % 4 < 2 else "a_q"] += both(at(lat, lon), at(lat + 1, lon))
        for lat in range(1, n_lat - 1, 2):
            for x, y in both((lat, lon), (lat + 1, lon)):
                p["b_p" if y[0] % 4 < 2 else "b_q"].append((at(*x), at(*y)))
            for x, y in both((lat, lon), (lat + 1, lon - 1)):
                p["k_p" if y[0] % 4 < 2 else "k_q"].append((at(*x), at(*y)))
        p["b_p"].append((at(n_lat - 1, lon), at(n_lat - 1, n_lon - 1 - lon)))
        p["k_p"].append((at(n_lat - 1, lon), at(n_lat - 1, n_lon - 2 - lon)))
    for lat in range(n_lat):
        side = "p" if lat % 4 < 2 else "q"
        for lon in range(0, n_lon, 2):
            p["c_" + side] += both(at(lat, lon), at(lat, lon + 1))
            p["d_" + side].append((at(lat, lon + 1), at(lat, lon + 2)))
            wraps = lon + 2 == n_lon
            p["d_q" if wraps else "d_" + side].append((at(lat, lon + 2), at(lat, lon + 1)))
    return p


def local(t, s, u, v, mix, depth):
    levels = t.shape[0]
    size = (lax.axis_size("lat"), lax.axis_size("lon"))
    total = float(size[0] * ROWS)
    pairs = exchanges(*size)
    flat = (levels * ROWS, LANES)
    rows, full = (4 * levels + 4, LANES), (levels, ROWS, LANES)
    column = (COL_ROWS, LANES)

    def send(x, name):
        return lax.ppermute(x, ("lon", "lat"), pairs[name])

    def bind(body, *args):
        return lambda *refs: body(size, levels, *args, *refs)

    *fields, depth, to_a, to_b, to_corner = call(
        bind(pack_rows), [x.reshape(flat) for x in (t, s, u, v)] + [depth], [],
        [flat] * 4 + [(ROWS, LANES), rows, rows, (ROWS, LANES)],
        [pltpu.VMEM((ROWS, LANES), jnp.int32), pltpu.SemaphoreType.DMA((5,))],
    )
    b_p = send(to_b, "b_p")
    k_p = send(to_corner, "k_p")
    a_p = send(to_a, "a_p")
    cols_p = call(bind(pack_columns, True), [], [*fields, depth, a_p], [column] * 2)
    d_p = send(cols_p[1], "d_p")
    c_p = send(cols_p[0], "c_p")
    work = call(bind(local_work, total, True), [], [*fields, mix, depth], [full] * 7)
    b_q = send(to_b, "b_q")
    k_q = send(to_corner, "k_q")
    a_q = send(to_a, "a_q")
    cols_q = call(bind(pack_columns, False), [], [*fields, depth, a_q, *cols_p], [column] * 2)
    d_q = send(cols_q[1], "d_q")
    c_q = send(cols_q[0], "c_q")
    work = call(
        bind(local_work, total, False), [], [*fields, mix, depth, *work], [full] * 7,
        aliases={6 + i: i for i in range(7)},
    )
    padded = (levels + 7) // 8 * 8
    return tuple(
        call(
            bind(finish, total), [],
            [*work, depth, to_a, to_b, a_p, a_q, b_p, b_q, *cols_q, c_p, d_p, c_q, d_q, k_p, k_q],
            [full] * 4,
            [
                pltpu.VMEM((5, padded, LANES), jnp.float32),
                pltpu.VMEM((4, padded, LANES), jnp.float32),
                pltpu.VMEM((4,) + full, jnp.float32),
            ],
            keep=False,
        )
    )


def solution(mesh):
    field = P(None, "lat", "lon")

    return jax.shard_map(
        local,
        mesh=mesh,
        in_specs=(field,) * 5 + (P("lat", "lon"),),
        out_specs=(field,) * 4,
        check_vma=False,
    )
```

```python
import jax
import jax.numpy as jnp
from jax import lax
from jax.experimental import pallas as pl
from jax.experimental.pallas import tpu as pltpu
from jax.sharding import PartitionSpec as P


DT = 0.2
CORIOLIS = 1.5
PRESSURE = 0.05
VISC_STEP = 0.1

ROWS, LANES = 8, 128
VMEM_GRANT = 8 << 20
UNROLL = 5
COL_ROWS = 40


def elimination_constants(levels):
    inner, last = [], []
    for k in range(levels):
        above = VISC_STEP * VISC_STEP * inner[k - 1] if k else 0.0
        step = VISC_STEP if k else 0.0
        inner.append(1.0 / (1.0 + step + VISC_STEP - above))
        last.append(1.0 / (1.0 + step - above))
    return inner, last


def lane_ids():
    return lax.broadcasted_iota(jnp.int32, (ROWS, LANES), 1)


def row_ids():
    return lax.broadcasted_iota(jnp.int32, (ROWS, LANES), 0)


def roll(x, shift, axis):
    return pltpu.roll(x, shift % x.shape[axis], axis)


def density_of(t, s):
    return -(1.0 + 0.1 * t) * t + 0.8 * s - 0.1 * t * s


def level_to_lane(rows, lane):
    k = lax.broadcasted_iota(jnp.int32, rows.shape, 0)
    l = lax.broadcasted_iota(jnp.int32, rows.shape, 1)
    return jnp.sum(jnp.where(k == l, rows[:, lane : lane + 1], 0.0), axis=0, keepdims=True)


def place_of(n_lat, n_lon):
    lat, lon = lax.axis_index("lat"), lax.axis_index("lon")
    first = lax.rem(lat, 4) < 2
    return lat, lon, first, jnp.logical_and(first, lon < n_lon // 2), lat == n_lat - 1


def pack_rows(mesh_size, levels, t, s, u, v, depth, t_out, s_out, u_out, v_out, h_out, to_a, to_b, corner, ints, sems):
    lat, _, _, _, _ = place_of(*mesh_size)
    even = lax.rem(lat, 2) == 0
    outs = (t_out, s_out, u_out, v_out)
    copies = [
        pltpu.make_async_copy(x, y, sems.at[f]) for f, (x, y) in enumerate(zip((t, s, u, v), outs))
    ]
    copies.append(pltpu.make_async_copy(depth, ints, sems.at[4]))
    for copy in copies:
        copy.start()
    copies[4].wait()
    h = ints[...].astype(jnp.float32)
    h_out[...] = h
    blank = jnp.zeros((3, LANES), jnp.float32)
    last = 4 * levels
    to_a[last : last + 4, :] = jnp.concatenate([jnp.where(even, h[7:8], h[0:1]), blank], axis=0)
    to_b[last : last + 4, :] = jnp.concatenate([jnp.where(even, h[0:1], h[7:8]), blank], axis=0)
    packed = []
    for f, ref in enumerate(outs):
        copies[f].wait()
        top = ref[pl.ds(ROWS - 1, levels, stride=ROWS), :]
        low = ref[pl.ds(0, levels, stride=ROWS), :]
        to_a[pl.ds(f, levels, stride=4), :] = jnp.where(even, top, low)
        b = jnp.where(even, low, top)
        to_b[pl.ds(f, levels, stride=4), :] = b
        packed.append(b)
    cu = level_to_lane(packed[2], LANES - 1)
    cv = level_to_lane(packed[3], 0)
    row = row_ids()
    corner[...] = jnp.where(row == 0, cu, jnp.where(row == 1, cv, 0.0))


def pack_columns(mesh_size, levels, early, t, s, u, v, depth, from_a, *refs):
    to_c, to_d = refs[-2:]
    lat, lon, first, _, _ = place_of(*mesh_size)
    lat_even = lax.rem(lat, 2) == 0
    lon_even = lax.rem(lon, 2) == 0
    if not early:

        @pl.when(first)
        def _():
            to_c[...] = refs[0][...]
            to_d[...] = refs[1][...]

    @pl.when(first if early else jnp.logical_not(first))
    def _():
        lane = lane_ids()
        h = depth[...]
        for f, ref in enumerate((t, s, u, v)):
            east = jnp.zeros((ROWS, LANES), jnp.float32)
            west = jnp.zeros((ROWS, LANES), jnp.float32)
            for k in range(levels):
                x = ref[k * ROWS : (k + 1) * ROWS, :]
                east = jnp.where(lane == k, x[:, LANES - 1 : LANES], east)
                west = jnp.where(lane == k, x[:, 0:1], west)
            if f == 0:
                east = jnp.where(lane == levels, h[:, LANES - 1 : LANES], east)
                west = jnp.where(lane == levels, h[:, 0:1], west)
            to_c[f * ROWS : (f + 1) * ROWS, :] = jnp.where(lon_even, east, west)
            to_d[f * ROWS : (f + 1) * ROWS, :] = jnp.where(lon_even, west, east)
        cu = level_to_lane(from_a[pl.ds(2, levels, stride=4), :], LANES - 1)
        cv = level_to_lane(from_a[pl.ds(3, levels, stride=4), :], 0)
        east = jnp.broadcast_to(jnp.where(lat_even, cu, 0.0), (ROWS, LANES))
        west = jnp.broadcast_to(jnp.where(lat_even, 0.0, cv), (ROWS, LANES))
        to_c[4 * ROWS : 5 * ROWS, :] = jnp.where(lon_even, east, west)
        to_d[4 * ROWS : 5 * ROWS, :] = jnp.where(lon_even, west, east)


def coriolis_rows(lat, total):
    row = (lat * ROWS + row_ids()).astype(jnp.float32)
    return CORIOLIS * (2.0 * (row + 0.5) / total - 1.0)


def local_work(mesh_size, levels, total, early, *refs):
    t, s, u, v, mix, depth = refs[:6]
    st, ss, su, sv, ra, aa, ba = refs[-7:]
    lat, _, _, soon, _ = place_of(*mesh_size)

    @pl.when(soon if early else jnp.logical_not(soon))
    def _():
        lane, row = lane_ids(), row_ids()
        h = depth[...]
        f4 = (0.25 * DT) * coriolis_rows(lat, total)
        open_e = jnp.where(lane < LANES - 1, jnp.minimum(h, roll(h, -1, 1)), 0.0)
        open_n = jnp.where(row < ROWS - 1, jnp.minimum(h, roll(h, -1, 0)), 0.0)
        zero = h - h
        one = zero + 1.0

        def level(k, carry):
            summed, c_here, minor, minor_prev = carry
            kf = jnp.asarray(k, jnp.float32)
            at = pl.ds(pl.multiple_of(k * ROWS, ROWS), ROWS)
            tk, sk, uk, vk = t[at, :], s[at, :], u[at, :], v[at, :]
            wet = h > kf
            dens = jnp.where(wet, PRESSURE * density_of(tk, sk), 0.0)
            summed = summed + dens
            p = summed - 0.5 * dens
            me, mn = open_e > kf, open_n > kf
            half_u, half_v = 0.5 * uk, 0.5 * vk
            e0, e1 = jnp.where(me, half_u + 0.5, 0.0), jnp.where(me, half_u - 0.5, 0.0)
            n0, n1 = jnp.where(mn, half_v + 0.5, 0.0), jnp.where(mn, half_v - 0.5, 0.0)
            for x, out in ((tk, st), (sk, ss)):
                fe = e0 * x + e1 * roll(x, -1, 1)
                fn = n0 * x + n1 * roll(x, -1, 0)
                out[k] = x - DT * (fe - roll(fe, 1, 1) + fn - roll(fn, 1, 0))
            uw, ve = roll(uk, 1, 1), roll(vk, -1, 1)
            un, vs = roll(uk, -1, 0), roll(vk, 1, 0)
            lap_u = (roll(uk, -1, 1) + uw) + (un + roll(uk, 1, 0)) - 4.0 * uk
            lap_v = (ve + roll(vk, 1, 1)) + (roll(vk, -1, 0) + vs) - 4.0 * vk
            v4 = (vk + ve) + (vs + roll(ve, 1, 0))
            u4 = (uk + uw) + (un + roll(uw, -1, 0))
            su[k] = uk + f4 * v4 - DT * (roll(p, -1, 1) - p) + 0.1 * lap_u
            sv[k] = vk - f4 * u4 - DT * (roll(p, -1, 0) - p) + 0.1 * lap_v
            below = mix[jnp.minimum(k, levels - 2)]
            c_next = jnp.where(h > kf + 1.0, DT * below, 0.0)
            minor_next = (1.0 + c_here + c_next) * minor - (c_here * c_here) * minor_prev
            r = jnp.where(wet, minor / minor_next, 0.0)
            ra[k] = r
            aa[k] = c_here * r
            ba[k] = c_next * r
            return summed, c_next, minor_next, minor

        lax.fori_loop(0, levels, level, (zero, zero, one, zero), unroll=UNROLL)


def finish(mesh_size, levels, total, *refs):
    (st, ss, su, sv, ra, aa, ba, depth, to_a, to_b, a_p, a_q, b_p, b_q, c_own, d_own,
     c_p, d_p, c_q, d_q, corner_p, corner_q, ot, os, ou, ov, north, south, kept) = refs
    lat, lon, first, _, top = place_of(*mesh_size)
    lane, row = lane_ids(), row_ids()
    lat_even = lax.rem(lat, 2) == 0
    lon_even = lax.rem(lon, 2) == 0
    b_first = jnp.logical_or(first, top)
    h = depth[...]
    f4 = (0.25 * DT) * coriolis_rows(lat, total)
    f7, f0 = f4[7:8, :], f4[0:1, :]

    kk = lax.broadcasted_iota(jnp.int32, (levels, LANES), 0).astype(jnp.float32)
    ll = lax.broadcasted_iota(jnp.int32, (levels, LANES), 1)

    def field(ref, f):
        return ref[pl.ds(f, levels, stride=4), :]

    def ghosts(f):
        a = jnp.where(first, field(a_p, f), field(a_q, f))
        b = jnp.where(b_first, field(b_p, f), field(b_q, f))
        return jnp.where(lat_even, a, b), jnp.where(lat_even, b, a)

    def own(f):
        a, b = field(to_a, f), field(to_b, f)
        return jnp.where(lat_even, a, b), jnp.where(lat_even, b, a)

    def mirrored(x, last):
        ids = lax.rem(last + LANES - lax.broadcasted_iota(jnp.int32, x.shape, 1), LANES)
        return jnp.take_along_axis(x, ids, axis=1)

    at = slice(4 * levels, 4 * levels + 1)
    h_a = jnp.where(first, a_p[at, :], a_q[at, :])
    h_b = jnp.where(b_first, b_p[at, :], b_q[at, :])
    h_n = jnp.broadcast_to(jnp.where(lat_even, h_a, h_b), (ROWS, LANES))
    h_n = jnp.where(top, mirrored(h_n, LANES - 1), h_n)[0:1, :]
    h_s = jnp.where(lat_even, h_b, h_a)
    (tn, ts), (sn, ss_), (un, us), (vn, vs) = (ghosts(f) for f in range(4))
    (t7, t0), (s7, s0), (u7, u0), (v7, v0) = (own(f) for f in range(4))
    tn = jnp.where(top, mirrored(tn, LANES - 1), tn)
    sn = jnp.where(top, mirrored(sn, LANES - 1), sn)
    vn = jnp.where(top, -mirrored(vn, LANES - 1), vn)
    un = jnp.where(top, -mirrored(un, LANES - 2), un)
    unw = roll(un, 1, 1)
    unw = jnp.where(ll > 0, unw - roll(u0, 1, 1), jnp.where(top, unw, 0.0))
    un = jnp.where(jnp.logical_and(top, ll == LANES - 1), 0.0, un) - u0
    mask = jnp.minimum(h[7:8, :], h_n) > kk
    north[0, :levels, :] = jnp.where(mask, -0.1 * (v7 * (t7 + tn) - (tn - t7)), 0.0)
    north[1, :levels, :] = jnp.where(mask, -0.1 * (v7 * (s7 + sn) - (sn - s7)), 0.0)
    north[2, :levels, :] = 0.1 * un
    north[3, :levels, :] = 0.1 * (vn - v0) - f7 * (un + unw)
    north[4, :levels, :] = (DT * PRESSURE) * (
        jnp.where(h_n > kk, density_of(tn, sn), 0.0)
        - jnp.where(h[0:1, :] > kk, density_of(t0, s0), 0.0)
    )
    mask = jnp.minimum(h[0:1, :], h_s) > kk
    south[0, :levels, :] = jnp.where(mask, 0.1 * (vs * (ts + t0) - (t0 - ts)), 0.0)
    south[1, :levels, :] = jnp.where(mask, 0.1 * (vs * (ss_ + s0) - (s0 - ss_)), 0.0)
    vs = vs - v7
    vse = jnp.where(ll < LANES - 1, roll(vs, -1, 1), 0.0)
    south[2, :levels, :] = 0.1 * (us - u7) + f0 * (vs + vse)
    south[3, :levels, :] = 0.1 * vs

    kl = lane.astype(jnp.float32)

    def tiles(c, d, f):
        at = slice(f * ROWS, (f + 1) * ROWS)
        x, y = c(at), d(at)
        return jnp.where(lon_even, x, y), jnp.where(lon_even, y, x)

    def got_c(at):
        return jnp.where(first, c_p[at, :], c_q[at, :])

    def got_d(at):
        return jnp.where(first, d_p[at, :], d_q[at, :])

    def own_c(at):
        return c_own[at, :]

    def own_d(at):
        return d_own[at, :]

    (te, tw), (se, sw), (ue, uw), (ve, vw), (ce, cw) = (tiles(got_c, got_d, f) for f in range(5))
    (t9, tz), (s9, sz), (u9, uz), (v9, vz) = (tiles(own_c, own_d, f) for f in range(4))
    cb = jnp.where(b_first, corner_p[...], corner_q[...])
    cb_u = jnp.broadcast_to(cb[0:1, :], (ROWS, LANES))
    cb_v = jnp.broadcast_to(cb[1:2, :], (ROWS, LANES))
    south_east = jnp.where(lat_even, cb_v, ce)
    north_west = jnp.where(lat_even, cw, jnp.where(top, 0.0, cb_u))
    north_end = jnp.where(jnp.logical_and(top, row == ROWS - 1), -cb_u, 0.0)
    h_e = te[:, levels : levels + 1]
    h_w = tw[:, levels : levels + 1]
    mask = jnp.minimum(h[:, LANES - 1 : LANES], h_e) > kl
    dt_e = jnp.where(mask, -0.1 * (u9 * (t9 + te) - (te - t9)), 0.0)
    ds_e = jnp.where(mask, -0.1 * (u9 * (s9 + se) - (se - s9)), 0.0)
    mask = jnp.minimum(h[:, 0:1], h_w) > kl
    dt_w = jnp.where(mask, 0.1 * (uw * (tw + tz) - (tz - tw)), 0.0)
    ds_w = jnp.where(mask, 0.1 * (uw * (sw + sz) - (sz - sw)), 0.0)
    dens = jnp.where(h_e > kl, density_of(te, se), 0.0) - jnp.where(
        h[:, 0:1] > kl, density_of(tz, sz), 0.0
    )
    summed = dens
    for step in (1, 2, 4, 8, 16, 32, 64):
        summed = summed + jnp.where(lane >= step, roll(summed, step, 1), 0.0)
    pe = (DT * PRESSURE) * (summed - 0.5 * dens)
    ve_up = jnp.where(row > 0, roll(ve, 1, 0), south_east) - roll(vz, 1, 0)
    uw_dn = jnp.where(row < ROWS - 1, roll(uw, -1, 0), north_west) - roll(u9, -1, 0)
    du_e = f4 * ((ve - vz) + ve_up) - pe + 0.1 * (ue - uz) + 0.1 * north_end
    du_w = 0.1 * (uw - u9)
    dv_e = 0.1 * (ve - vz) - f4 * north_end
    dv_w = 0.1 * (vw - v9) - f4 * ((uw - u9) + uw_dn)

    m_u = jnp.minimum(h, jnp.where(lane < LANES - 1, roll(h, -1, 1), h_e))
    m_v = jnp.minimum(h, jnp.where(row < ROWS - 1, roll(h, -1, 0), h_n))
    at_n, at_s = row == ROWS - 1, row == 0
    at_e, at_w = lane == LANES - 1, lane == 0
    inner, last = elimination_constants(levels)
    head = levels % UNROLL + UNROLL
    sides = ((dt_e, dt_w), (ds_e, ds_w), (du_e, du_w), (dv_e, dv_w))

    def down(k, c, carry):
        pt, ps, pu, pv, cs = carry
        kf = jnp.asarray(k, jnp.float32)
        one = pl.ds(k, 1)

        def spread(f, extra=None):
            n = north[f, one, :]
            if extra is not None:
                n = n - extra
            base = jnp.where(at_n, n, jnp.where(at_s, south[f, one, :], 0.0))
            de = pltpu.roll(sides[f][0], LANES - 1 - k, 1)
            dw = pltpu.roll(sides[f][1], lax.rem(LANES - k, LANES), 1)
            return base + jnp.where(at_e, de, jnp.where(at_w, dw, 0.0))

        dn = north[4, one, :]
        cs = cs + dn
        r, a = ra[k], aa[k]
        ru = jnp.where(m_u > kf + 1.0, inner[c], jnp.where(m_u > kf, last[c], 0.0))
        rv = jnp.where(m_v > kf + 1.0, inner[c], jnp.where(m_v > kf, last[c], 0.0))
        pt = r * (st[k] + spread(0)) + a * pt
        ps = r * (ss[k] + spread(1)) + a * ps
        pu = ru * (su[k] + spread(2)) + (VISC_STEP * ru) * pu
        pv = rv * (sv[k] + spread(3, cs - 0.5 * dn)) + (VISC_STEP * rv) * pv
        for f, x in enumerate((pt, ps, pu, pv)):
            kept[f, k] = x
        return pt, ps, pu, pv, cs

    def up(k, c, carry):
        xt, xs, xu, xv = carry
        kf = jnp.asarray(k, jnp.float32)
        b = ba[k]
        bu = jnp.where(m_u > kf + 1.0, VISC_STEP * inner[c], 0.0)
        bv = jnp.where(m_v > kf + 1.0, VISC_STEP * inner[c], 0.0)
        xt = kept[0, k] + b * xt
        xs = kept[1, k] + b * xs
        xu = kept[2, k] + bu * xu
        xv = kept[3, k] + bv * xv
        ot[k], os[k], ou[k], ov[k] = xt, xs, xu, xv
        return xt, xs, xu, xv

    zero = h - h
    carry = (zero, zero, zero, zero, zero[0:1, :])
    for k in range(head):
        carry = down(k, k, carry)
    carry = lax.fori_loop(head, levels, lambda k, x: down(k, head, x), carry, unroll=UNROLL)
    carry = lax.fori_loop(
        head, levels, lambda i, x: up(levels - 1 + head - i, head, x), (zero,) * 4, unroll=UNROLL
    )
    for k in range(head - 1, -1, -1):
        carry = up(k, k, carry)


HBM = pl.BlockSpec(memory_space=pltpu.HBM)
VMEM = pl.BlockSpec(memory_space=pltpu.VMEM)


def call(body, far, near, outs, scratch=(), aliases=None, keep=True):
    far = [pltpu.with_memory_space_constraint(x, pltpu.HBM) for x in far]
    near = [pltpu.with_memory_space_constraint(x, pltpu.VMEM) for x in near]
    shapes = tuple(
        pltpu.VMEM(s, jnp.float32) if keep else jax.ShapeDtypeStruct(s, jnp.float32) for s in outs
    )
    return pl.pallas_call(
        body,
        out_shape=shapes,
        in_specs=[HBM] * len(far) + [VMEM] * len(near),
        out_specs=tuple(VMEM for _ in outs),
        scratch_shapes=list(scratch),
        input_output_aliases=aliases or {},
        compiler_params=pltpu.CompilerParams(vmem_limit_bytes=VMEM_GRANT),
    )(*far, *near)


def exchanges(n_lat, n_lon):
    def at(lat, lon):
        return (lon % n_lon) * n_lat + lat

    def both(x, y):
        return [(x, y), (y, x)]

    p = {name: [] for name in [x + y for x in "abkcd" for y in ("_p", "_q")]}
    for lon in range(n_lon):
        for lat in range(0, n_lat, 2):
            p["a_p" if lat % 4 < 2 else "a_q"] += both(at(lat, lon), at(lat + 1, lon))
        for lat in range(1, n_lat - 1, 2):
            for x, y in both((lat, lon), (lat + 1, lon)):
                p["b_p" if y[0] % 4 < 2 else "b_q"].append((at(*x), at(*y)))
            for x, y in both((lat, lon), (lat + 1, lon - 1)):
                p["k_p" if y[0] % 4 < 2 else "k_q"].append((at(*x), at(*y)))
        p["b_p"].append((at(n_lat - 1, lon), at(n_lat - 1, n_lon - 1 - lon)))
        p["k_p"].append((at(n_lat - 1, lon), at(n_lat - 1, n_lon - 2 - lon)))
    for lat in range(n_lat):
        side = "p" if lat % 4 < 2 else "q"
        for lon in range(0, n_lon, 2):
            p["c_" + side] += both(at(lat, lon), at(lat, lon + 1))
            p["d_" + side] += both(at(lat, lon + 1), at(lat, lon + 2))
    return p


def local(t, s, u, v, mix, depth):
    levels = t.shape[0]
    size = (lax.axis_size("lat"), lax.axis_size("lon"))
    total = float(size[0] * ROWS)
    pairs = exchanges(*size)
    flat = (levels * ROWS, LANES)
    rows, full = (4 * levels + 4, LANES), (levels, ROWS, LANES)
    column = (COL_ROWS, LANES)

    def send(x, name):
        return lax.ppermute(x, ("lon", "lat"), pairs[name])

    def bind(body, *args):
        return lambda *refs: body(size, levels, *args, *refs)

    *fields, depth, to_a, to_b, to_corner = call(
        bind(pack_rows), [x.reshape(flat) for x in (t, s, u, v)] + [depth], [],
        [flat] * 4 + [(ROWS, LANES), rows, rows, (ROWS, LANES)],
        [pltpu.VMEM((ROWS, LANES), jnp.int32), pltpu.SemaphoreType.DMA((5,))],
    )
    b_p = send(to_b, "b_p")
    k_p = send(to_corner, "k_p")
    a_p = send(to_a, "a_p")
    cols_p = call(bind(pack_columns, True), [], [*fields, depth, a_p], [column] * 2)
    d_p = send(cols_p[1], "d_p")
    c_p = send(cols_p[0], "c_p")
    work = call(bind(local_work, total, True), [], [*fields, mix, depth], [full] * 7)
    b_q = send(to_b, "b_q")
    k_q = send(to_corner, "k_q")
    a_q = send(to_a, "a_q")
    cols_q = call(bind(pack_columns, False), [], [*fields, depth, a_q, *cols_p], [column] * 2)
    d_q = send(cols_q[1], "d_q")
    c_q = send(cols_q[0], "c_q")
    work = call(
        bind(local_work, total, False), [], [*fields, mix, depth, *work], [full] * 7,
        aliases={6 + i: i for i in range(7)},
    )
    padded = (levels + 7) // 8 * 8
    return tuple(
        call(
            bind(finish, total), [],
            [*work, depth, to_a, to_b, a_p, a_q, b_p, b_q, *cols_q, c_p, d_p, c_q, d_q, k_p, k_q],
            [full] * 4,
            [
                pltpu.VMEM((5, padded, LANES), jnp.float32),
                pltpu.VMEM((4, padded, LANES), jnp.float32),
                pltpu.VMEM((4,) + full, jnp.float32),
            ],
            keep=False,
        )
    )


def solution(mesh):
    field = P(None, "lat", "lon")

    return jax.shard_map(
        local,
        mesh=mesh,
        in_specs=(field,) * 5 + (P("lat", "lon"),),
        out_specs=(field,) * 4,
        check_vma=False,
    )
```

```python
import jax
import jax.numpy as jnp
from jax import lax
from jax.experimental import pallas as pl
from jax.experimental.pallas import tpu as pltpu
from jax.sharding import PartitionSpec as P


DT = 0.2
CORIOLIS = 1.5
PRESSURE = 0.05
VISC_STEP = 0.1

ROWS, LANES = 8, 128
VMEM_GRANT = 8 << 20
UNROLL = 5
COL_ROWS = 40


def elimination_constants(levels):
    inner, last = [], []
    for k in range(levels):
        above = VISC_STEP * VISC_STEP * inner[k - 1] if k else 0.0
        step = VISC_STEP if k else 0.0
        inner.append(1.0 / (1.0 + step + VISC_STEP - above))
        last.append(1.0 / (1.0 + step - above))
    return inner, last


def lane_ids():
    return lax.broadcasted_iota(jnp.int32, (ROWS, LANES), 1)


def row_ids():
    return lax.broadcasted_iota(jnp.int32, (ROWS, LANES), 0)


def roll(x, shift, axis):
    return pltpu.roll(x, shift % x.shape[axis], axis)


def density_of(t, s):
    return -(1.0 + 0.1 * t) * t + 0.8 * s - 0.1 * t * s


def level_to_lane(rows, lane):
    k = lax.broadcasted_iota(jnp.int32, rows.shape, 0)
    l = lax.broadcasted_iota(jnp.int32, rows.shape, 1)
    return jnp.sum(jnp.where(k == l, rows[:, lane : lane + 1], 0.0), axis=0, keepdims=True)


def place_of(n_lat, n_lon):
    lat, lon = lax.axis_index("lat"), lax.axis_index("lon")
    first = lax.rem(lat, 4) < 2
    return lat, lon, first, jnp.logical_and(first, lon < n_lon // 2), lat == n_lat - 1


def pack_rows(mesh_size, levels, t, s, u, v, depth, t_out, s_out, u_out, v_out, h_out, to_a, to_b, corner, ints, sems):
    lat, _, _, _, _ = place_of(*mesh_size)
    even = lax.rem(lat, 2) == 0
    outs = (t_out, s_out, u_out, v_out)
    copies = [
        pltpu.make_async_copy(x, y, sems.at[f]) for f, (x, y) in enumerate(zip((t, s, u, v), outs))
    ]
    copies.append(pltpu.make_async_copy(depth, ints, sems.at[4]))
    for copy in copies:
        copy.start()
    copies[4].wait()
    h = ints[...].astype(jnp.float32)
    h_out[...] = h
    blank = jnp.zeros((3, LANES), jnp.float32)
    last = 4 * levels
    to_a[last : last + 4, :] = jnp.concatenate([jnp.where(even, h[7:8], h[0:1]), blank], axis=0)
    to_b[last : last + 4, :] = jnp.concatenate([jnp.where(even, h[0:1], h[7:8]), blank], axis=0)
    packed = []
    for f, ref in enumerate(outs):
        copies[f].wait()
        top = ref[pl.ds(ROWS - 1, levels, stride=ROWS), :]
        low = ref[pl.ds(0, levels, stride=ROWS), :]
        to_a[pl.ds(f, levels, stride=4), :] = jnp.where(even, top, low)
        b = jnp.where(even, low, top)
        to_b[pl.ds(f, levels, stride=4), :] = b
        packed.append(b)
    cu = level_to_lane(packed[2], LANES - 1)
    cv = level_to_lane(packed[3], 0)
    row = row_ids()
    corner[...] = jnp.where(row == 0, cu, jnp.where(row == 1, cv, 0.0))


def pack_columns(mesh_size, levels, early, t, s, u, v, depth, from_a, *refs):
    to_c, to_d = refs[-2:]
    lat, lon, first, _, _ = place_of(*mesh_size)
    lat_even = lax.rem(lat, 2) == 0
    lon_even = lax.rem(lon, 2) == 0
    if not early:

        @pl.when(first)
        def _():
            to_c[...] = refs[0][...]
            to_d[...] = refs[1][...]

    @pl.when(first if early else jnp.logical_not(first))
    def _():
        lane = lane_ids()
        h = depth[...]
        for f, ref in enumerate((t, s, u, v)):
            east = jnp.zeros((ROWS, LANES), jnp.float32)
            west = jnp.zeros((ROWS, LANES), jnp.float32)
            for k in range(levels):
                x = ref[k * ROWS : (k + 1) * ROWS, :]
                east = jnp.where(lane == k, roll(x, k + 1, 1), east)
                west = jnp.where(lane == k, roll(x, k, 1), west)
            if f == 0:
                east = jnp.where(lane == levels, h[:, LANES - 1 : LANES], east)
                west = jnp.where(lane == levels, h[:, 0:1], west)
            to_c[f * ROWS : (f + 1) * ROWS, :] = jnp.where(lon_even, east, west)
            to_d[f * ROWS : (f + 1) * ROWS, :] = jnp.where(lon_even, west, east)
        cu = level_to_lane(from_a[pl.ds(2, levels, stride=4), :], LANES - 1)
        cv = level_to_lane(from_a[pl.ds(3, levels, stride=4), :], 0)
        east = jnp.broadcast_to(jnp.where(lat_even, cu, 0.0), (ROWS, LANES))
        west = jnp.broadcast_to(jnp.where(lat_even, 0.0, cv), (ROWS, LANES))
        to_c[4 * ROWS : 5 * ROWS, :] = jnp.where(lon_even, east, west)
        to_d[4 * ROWS : 5 * ROWS, :] = jnp.where(lon_even, west, east)


def pack_far(mesh_size, levels, to_b, from_c, from_d, out):
    lat, lon, first, _, _ = place_of(*mesh_size)
    lon_even = lax.rem(lon, 2) == 0

    @pl.when(first)
    def _():
        out[...] = to_b[...]
        v_east = jnp.where(lon_even, from_c[4 * ROWS - 1 : 4 * ROWS, :], from_d[4 * ROWS - 1 : 4 * ROWS, :])
        u_west = jnp.where(lon_even, from_d[2 * ROWS : 2 * ROWS + 1, :], from_c[2 * ROWS : 2 * ROWS + 1, :])
        at = 4 * levels + 1
        out[at : at + 1, :] = jnp.where(lax.rem(lat, 2) == 0, u_west, v_east)


def coriolis_rows(lat, total):
    row = (lat * ROWS + row_ids()).astype(jnp.float32)
    return CORIOLIS * (2.0 * (row + 0.5) / total - 1.0)


def local_work(mesh_size, levels, total, early, *refs):
    t, s, u, v, mix, depth = refs[:6]
    st, ss, su, sv, ra, aa, ba = refs[-7:]
    lat, _, _, soon, _ = place_of(*mesh_size)

    @pl.when(soon if early else jnp.logical_not(soon))
    def _():
        lane, row = lane_ids(), row_ids()
        h = depth[...]
        f4 = (0.25 * DT) * coriolis_rows(lat, total)
        open_e = jnp.where(lane < LANES - 1, jnp.minimum(h, roll(h, -1, 1)), 0.0)
        open_n = jnp.where(row < ROWS - 1, jnp.minimum(h, roll(h, -1, 0)), 0.0)
        zero = h - h
        one = zero + 1.0

        def level(k, carry):
            summed, c_here, minor, minor_prev = carry
            kf = jnp.asarray(k, jnp.float32)
            at = pl.ds(pl.multiple_of(k * ROWS, ROWS), ROWS)
            tk, sk, uk, vk = t[at, :], s[at, :], u[at, :], v[at, :]
            wet = h > kf
            dens = jnp.where(wet, PRESSURE * density_of(tk, sk), 0.0)
            summed = summed + dens
            p = summed - 0.5 * dens
            me, mn = open_e > kf, open_n > kf
            half_u, half_v = 0.5 * uk, 0.5 * vk
            e0, e1 = jnp.where(me, half_u + 0.5, 0.0), jnp.where(me, half_u - 0.5, 0.0)
            n0, n1 = jnp.where(mn, half_v + 0.5, 0.0), jnp.where(mn, half_v - 0.5, 0.0)
            for x, out in ((tk, st), (sk, ss)):
                fe = e0 * x + e1 * roll(x, -1, 1)
                fn = n0 * x + n1 * roll(x, -1, 0)
                out[k] = x - DT * (fe - roll(fe, 1, 1) + fn - roll(fn, 1, 0))
            uw, ve = roll(uk, 1, 1), roll(vk, -1, 1)
            un, vs = roll(uk, -1, 0), roll(vk, 1, 0)
            lap_u = (roll(uk, -1, 1) + uw) + (un + roll(uk, 1, 0)) - 4.0 * uk
            lap_v = (ve + roll(vk, 1, 1)) + (roll(vk, -1, 0) + vs) - 4.0 * vk
            v4 = (vk + ve) + (vs + roll(ve, 1, 0))
            u4 = (uk + uw) + (un + roll(uw, -1, 0))
            su[k] = uk + f4 * v4 - DT * (roll(p, -1, 1) - p) + 0.1 * lap_u
            sv[k] = vk - f4 * u4 - DT * (roll(p, -1, 0) - p) + 0.1 * lap_v
            below = mix[jnp.minimum(k, levels - 2)]
            c_next = jnp.where(h > kf + 1.0, DT * below, 0.0)
            minor_next = (1.0 + c_here + c_next) * minor - (c_here * c_here) * minor_prev
            r = jnp.where(wet, minor / minor_next, 0.0)
            ra[k] = r
            aa[k] = c_here * r
            ba[k] = c_next * r
            return summed, c_next, minor_next, minor

        lax.fori_loop(0, levels, level, (zero, zero, one, zero), unroll=UNROLL)


def finish(mesh_size, levels, total, *refs):
    (st, ss, su, sv, ra, aa, ba, depth, to_a, to_b, a_p, a_q, b_p, b_q, c_own, d_own,
     c_p, d_p, c_q, d_q, corner, ot, os, ou, ov, north, south, kept) = refs
    lat, lon, first, _, top = place_of(*mesh_size)
    lane, row = lane_ids(), row_ids()
    lat_even = lax.rem(lat, 2) == 0
    lon_even = lax.rem(lon, 2) == 0
    b_first = jnp.logical_or(first, top)
    h = depth[...]
    f4 = (0.25 * DT) * coriolis_rows(lat, total)
    f7, f0 = f4[7:8, :], f4[0:1, :]

    kk = lax.broadcasted_iota(jnp.int32, (levels, LANES), 0).astype(jnp.float32)
    ll = lax.broadcasted_iota(jnp.int32, (levels, LANES), 1)

    def field(ref, f):
        return ref[pl.ds(f, levels, stride=4), :]

    def ghosts(f):
        a = jnp.where(first, field(a_p, f), field(a_q, f))
        b = jnp.where(b_first, field(b_p, f), field(b_q, f))
        return jnp.where(lat_even, a, b), jnp.where(lat_even, b, a)

    def own(f):
        a, b = field(to_a, f), field(to_b, f)
        return jnp.where(lat_even, a, b), jnp.where(lat_even, b, a)

    def mirrored(x, last):
        ids = lax.rem(last + LANES - lax.broadcasted_iota(jnp.int32, x.shape, 1), LANES)
        return jnp.take_along_axis(x, ids, axis=1)

    at = slice(4 * levels, 4 * levels + 1)
    h_a = jnp.where(first, a_p[at, :], a_q[at, :])
    h_b = jnp.where(b_first, b_p[at, :], b_q[at, :])
    h_n = jnp.broadcast_to(jnp.where(lat_even, h_a, h_b), (ROWS, LANES))
    h_n = jnp.where(top, mirrored(h_n, LANES - 1), h_n)[0:1, :]
    h_s = jnp.where(lat_even, h_b, h_a)
    (tn, ts), (sn, ss_), (un, us), (vn, vs) = (ghosts(f) for f in range(4))
    (t7, t0), (s7, s0), (u7, u0), (v7, v0) = (own(f) for f in range(4))
    tn = jnp.where(top, mirrored(tn, LANES - 1), tn)
    sn = jnp.where(top, mirrored(sn, LANES - 1), sn)
    vn = jnp.where(top, -mirrored(vn, LANES - 1), vn)
    un = jnp.where(top, -mirrored(un, LANES - 2), un)
    unw = roll(un, 1, 1)
    unw = jnp.where(ll > 0, unw - roll(u0, 1, 1), jnp.where(top, unw, 0.0))
    un = jnp.where(jnp.logical_and(top, ll == LANES - 1), 0.0, un) - u0
    mask = jnp.minimum(h[7:8, :], h_n) > kk
    north[0, :levels, :] = jnp.where(mask, -0.1 * (v7 * (t7 + tn) - (tn - t7)), 0.0)
    north[1, :levels, :] = jnp.where(mask, -0.1 * (v7 * (s7 + sn) - (sn - s7)), 0.0)
    north[2, :levels, :] = 0.1 * un
    north[3, :levels, :] = 0.1 * (vn - v0) - f7 * (un + unw)
    north[4, :levels, :] = (DT * PRESSURE) * (
        jnp.where(h_n > kk, density_of(tn, sn), 0.0)
        - jnp.where(h[0:1, :] > kk, density_of(t0, s0), 0.0)
    )
    mask = jnp.minimum(h[0:1, :], h_s) > kk
    south[0, :levels, :] = jnp.where(mask, 0.1 * (vs * (ts + t0) - (t0 - ts)), 0.0)
    south[1, :levels, :] = jnp.where(mask, 0.1 * (vs * (ss_ + s0) - (s0 - ss_)), 0.0)
    vs = vs - v7
    vse = jnp.where(ll < LANES - 1, roll(vs, -1, 1), 0.0)
    south[2, :levels, :] = 0.1 * (us - u7) + f0 * (vs + vse)
    south[3, :levels, :] = 0.1 * vs

    kl = lane.astype(jnp.float32)

    def tiles(c, d, f):
        at = slice(f * ROWS, (f + 1) * ROWS)
        x, y = c(at), d(at)
        return jnp.where(lon_even, x, y), jnp.where(lon_even, y, x)

    def got_c(at):
        return jnp.where(first, c_p[at, :], c_q[at, :])

    def got_d(at):
        return jnp.where(first, d_p[at, :], d_q[at, :])

    def own_c(at):
        return c_own[at, :]

    def own_d(at):
        return d_own[at, :]

    (te, tw), (se, sw), (ue, uw), (ve, vw), (ce, cw) = (tiles(got_c, got_d, f) for f in range(5))
    (t9, tz), (s9, sz), (u9, uz), (v9, vz) = (tiles(own_c, own_d, f) for f in range(4))
    late = b_q[4 * levels + 1 : 4 * levels + 2, :]
    cb_u = jnp.broadcast_to(jnp.where(b_first, corner[0:1, :], late), (ROWS, LANES))
    cb_v = jnp.broadcast_to(jnp.where(b_first, corner[1:2, :], late), (ROWS, LANES))
    south_east = jnp.where(lat_even, cb_v, ce)
    north_west = jnp.where(lat_even, cw, jnp.where(top, 0.0, cb_u))
    north_end = jnp.where(jnp.logical_and(top, row == ROWS - 1), -cb_u, 0.0)
    h_e = te[:, levels : levels + 1]
    h_w = tw[:, levels : levels + 1]
    mask = jnp.minimum(h[:, LANES - 1 : LANES], h_e) > kl
    dt_e = jnp.where(mask, -0.1 * (u9 * (t9 + te) - (te - t9)), 0.0)
    ds_e = jnp.where(mask, -0.1 * (u9 * (s9 + se) - (se - s9)), 0.0)
    mask = jnp.minimum(h[:, 0:1], h_w) > kl
    dt_w = jnp.where(mask, 0.1 * (uw * (tw + tz) - (tz - tw)), 0.0)
    ds_w = jnp.where(mask, 0.1 * (uw * (sw + sz) - (sz - sw)), 0.0)
    dens = jnp.where(h_e > kl, density_of(te, se), 0.0) - jnp.where(
        h[:, 0:1] > kl, density_of(tz, sz), 0.0
    )
    summed = dens
    for step in (1, 2, 4, 8, 16, 32, 64):
        summed = summed + jnp.where(lane >= step, roll(summed, step, 1), 0.0)
    pe = (DT * PRESSURE) * (summed - 0.5 * dens)
    ve_up = jnp.where(row > 0, roll(ve, 1, 0), south_east) - roll(vz, 1, 0)
    uw_dn = jnp.where(row < ROWS - 1, roll(uw, -1, 0), north_west) - roll(u9, -1, 0)
    du_e = f4 * ((ve - vz) + ve_up) - pe + 0.1 * (ue - uz) + 0.1 * north_end
    du_w = 0.1 * (uw - u9)
    dv_e = 0.1 * (ve - vz) - f4 * north_end
    dv_w = 0.1 * (vw - v9) - f4 * ((uw - u9) + uw_dn)

    m_u = jnp.minimum(h, jnp.where(lane < LANES - 1, roll(h, -1, 1), h_e))
    m_v = jnp.minimum(h, jnp.where(row < ROWS - 1, roll(h, -1, 0), h_n))
    at_n, at_s = row == ROWS - 1, row == 0
    at_e, at_w = lane == LANES - 1, lane == 0
    inner, last = elimination_constants(levels)
    sides = ((dt_e, dt_w), (ds_e, ds_w), (du_e, du_w), (dv_e, dv_w))

    def down(k, c, carry):
        pt, ps, pu, pv, cs = carry
        kf = jnp.asarray(k, jnp.float32)
        one = pl.ds(k, 1)

        def spread(f, extra=None):
            n = north[f, one, :]
            if extra is not None:
                n = n - extra
            base = jnp.where(at_n, n, jnp.where(at_s, south[f, one, :], 0.0))
            de = pltpu.roll(sides[f][0], LANES - 1 - k, 1)
            dw = pltpu.roll(sides[f][1], (LANES - k) % LANES, 1)
            return base + jnp.where(at_e, de, jnp.where(at_w, dw, 0.0))

        dn = north[4, one, :]
        cs = cs + dn
        r, a = ra[k], aa[k]
        ru = jnp.where(m_u > kf + 1.0, inner[c], jnp.where(m_u > kf, last[c], 0.0))
        rv = jnp.where(m_v > kf + 1.0, inner[c], jnp.where(m_v > kf, last[c], 0.0))
        pt = r * (st[k] + spread(0)) + a * pt
        ps = r * (ss[k] + spread(1)) + a * ps
        pu = ru * (su[k] + spread(2)) + (VISC_STEP * ru) * pu
        pv = rv * (sv[k] + spread(3, cs - 0.5 * dn)) + (VISC_STEP * rv) * pv
        for f, x in enumerate((pt, ps, pu, pv)):
            kept[f, k] = x
        return pt, ps, pu, pv, cs

    def up(k, c, carry):
        xt, xs, xu, xv = carry
        kf = jnp.asarray(k, jnp.float32)
        b = ba[k]
        bu = jnp.where(m_u > kf + 1.0, VISC_STEP * inner[c], 0.0)
        bv = jnp.where(m_v > kf + 1.0, VISC_STEP * inner[c], 0.0)
        xt = kept[0, k] + b * xt
        xs = kept[1, k] + b * xs
        xu = kept[2, k] + bu * xu
        xv = kept[3, k] + bv * xv
        ot[k], os[k], ou[k], ov[k] = xt, xs, xu, xv
        return xt, xs, xu, xv

    zero = h - h
    carry = (zero, zero, zero, zero, zero[0:1, :])
    for k in range(levels):
        carry = down(k, k, carry)
    carry = (zero,) * 4
    for k in range(levels - 1, -1, -1):
        carry = up(k, k, carry)


HBM = pl.BlockSpec(memory_space=pltpu.HBM)
VMEM = pl.BlockSpec(memory_space=pltpu.VMEM)


def call(body, far, near, outs, scratch=(), aliases=None, keep=True):
    far = [pltpu.with_memory_space_constraint(x, pltpu.HBM) for x in far]
    near = [pltpu.with_memory_space_constraint(x, pltpu.VMEM) for x in near]
    shapes = tuple(
        pltpu.VMEM(s, jnp.float32) if keep else jax.ShapeDtypeStruct(s, jnp.float32) for s in outs
    )
    return pl.pallas_call(
        body,
        out_shape=shapes,
        in_specs=[HBM] * len(far) + [VMEM] * len(near),
        out_specs=tuple(VMEM for _ in outs),
        scratch_shapes=list(scratch),
        input_output_aliases=aliases or {},
        compiler_params=pltpu.CompilerParams(vmem_limit_bytes=VMEM_GRANT),
    )(*far, *near)


def exchanges(n_lat, n_lon):
    def at(lat, lon):
        return (lon % n_lon) * n_lat + lat

    def both(x, y):
        return [(x, y), (y, x)]

    p = {name: [] for name in [x + y for x in "abkcd" for y in ("_p", "_q")]}
    for lon in range(n_lon):
        for lat in range(0, n_lat, 2):
            p["a_p" if lat % 4 < 2 else "a_q"] += both(at(lat, lon), at(lat + 1, lon))
        for lat in range(1, n_lat - 1, 2):
            for x, y in both((lat, lon), (lat + 1, lon)):
                p["b_p" if y[0] % 4 < 2 else "b_q"].append((at(*x), at(*y)))
            for x, y in both((lat, lon), (lat + 1, lon - 1)):
                if y[0] % 4 < 2:
                    p["k_p"].append((at(*x), at(*y)))
        p["b_p"].append((at(n_lat - 1, lon), at(n_lat - 1, n_lon - 1 - lon)))
        p["k_p"].append((at(n_lat - 1, lon), at(n_lat - 1, n_lon - 2 - lon)))
    for lat in range(n_lat):
        side = "p" if lat % 4 < 2 else "q"
        for lon in range(0, n_lon, 2):
            p["c_" + side] += both(at(lat, lon), at(lat, lon + 1))
            p["d_" + side] += both(at(lat, lon + 1), at(lat, lon + 2))
    return p


def local(t, s, u, v, mix, depth):
    levels = t.shape[0]
    size = (lax.axis_size("lat"), lax.axis_size("lon"))
    total = float(size[0] * ROWS)
    pairs = exchanges(*size)
    flat = (levels * ROWS, LANES)
    rows, full = (4 * levels + 4, LANES), (levels, ROWS, LANES)
    column = (COL_ROWS, LANES)

    def send(x, name):
        return lax.ppermute(x, ("lon", "lat"), pairs[name])

    def bind(body, *args):
        return lambda *refs: body(size, levels, *args, *refs)

    *fields, depth, to_a, to_b, to_corner = call(
        bind(pack_rows), [x.reshape(flat) for x in (t, s, u, v)] + [depth], [],
        [flat] * 4 + [(ROWS, LANES), rows, rows, (ROWS, LANES)],
        [pltpu.VMEM((ROWS, LANES), jnp.int32), pltpu.SemaphoreType.DMA((5,))],
    )
    b_p = send(to_b, "b_p")
    k_p = send(to_corner, "k_p")
    a_p = send(to_a, "a_p")
    cols_p = call(bind(pack_columns, True), [], [*fields, depth, a_p], [column] * 2)
    d_p = send(cols_p[1], "d_p")
    c_p = send(cols_p[0], "c_p")
    work = call(bind(local_work, total, True), [], [*fields, mix, depth], [full] * 7)
    (to_far,) = call(bind(pack_far), [], [to_b, c_p, d_p], [rows])
    b_q = send(to_far, "b_q")
    a_q = send(to_a, "a_q")
    cols_q = call(bind(pack_columns, False), [], [*fields, depth, a_q, *cols_p], [column] * 2)
    d_q = send(cols_q[1], "d_q")
    c_q = send(cols_q[0], "c_q")
    work = call(
        bind(local_work, total, False), [], [*fields, mix, depth, *work], [full] * 7,
        aliases={6 + i: i for i in range(7)},
    )
    padded = (levels + 7) // 8 * 8
    return tuple(
        call(
            bind(finish, total), [],
            [*work, depth, to_a, to_b, a_p, a_q, b_p, b_q, *cols_q, c_p, d_p, c_q, d_q, k_p],
            [full] * 4,
            [
                pltpu.VMEM((5, padded, LANES), jnp.float32),
                pltpu.VMEM((4, padded, LANES), jnp.float32),
                pltpu.VMEM((4,) + full, jnp.float32),
            ],
            keep=False,
        )
    )


def solution(mesh):
    field = P(None, "lat", "lon")

    return jax.shard_map(
        local,
        mesh=mesh,
        in_specs=(field,) * 5 + (P("lat", "lon"),),
        out_specs=(field,) * 4,
        check_vma=False,
    )
```

```python
import jax
import jax.numpy as jnp
from jax import lax
from jax.experimental import pallas as pl
from jax.experimental.pallas import tpu as pltpu
from jax.sharding import PartitionSpec as P


DT = 0.2
CORIOLIS = 1.5
PRESSURE = 0.05
VISC_STEP = 0.1

ROWS, LANES = 8, 128
VMEM_GRANT = 8 << 20
UNROLL = 5
COL_ROWS = 40


def elimination_constants(levels):
    inner, last = [], []
    for k in range(levels):
        above = VISC_STEP * VISC_STEP * inner[k - 1] if k else 0.0
        step = VISC_STEP if k else 0.0
        inner.append(1.0 / (1.0 + step + VISC_STEP - above))
        last.append(1.0 / (1.0 + step - above))
    return inner, last


def lane_ids():
    return lax.broadcasted_iota(jnp.int32, (ROWS, LANES), 1)


def row_ids():
    return lax.broadcasted_iota(jnp.int32, (ROWS, LANES), 0)


def roll(x, shift, axis):
    return pltpu.roll(x, shift % x.shape[axis], axis)


def density_of(t, s):
    return -(1.0 + 0.1 * t) * t + 0.8 * s - 0.1 * t * s


def level_to_lane(rows, lane):
    k = lax.broadcasted_iota(jnp.int32, rows.shape, 0)
    l = lax.broadcasted_iota(jnp.int32, rows.shape, 1)
    return jnp.sum(jnp.where(k == l, rows[:, lane : lane + 1], 0.0), axis=0, keepdims=True)


def place_of(n_lat, n_lon):
    lat, lon = lax.axis_index("lat"), lax.axis_index("lon")
    first = lax.rem(lat, 4) < 2
    return lat, lon, first, jnp.logical_and(first, lon < n_lon // 2), lat == n_lat - 1


def pack_rows(mesh_size, levels, t, s, u, v, depth, t_out, s_out, u_out, v_out, h_out, to_a, to_b, corner, ints, sems):
    lat, _, _, _, _ = place_of(*mesh_size)
    even = lax.rem(lat, 2) == 0
    outs = (t_out, s_out, u_out, v_out)
    copies = [
        pltpu.make_async_copy(x, y, sems.at[f]) for f, (x, y) in enumerate(zip((t, s, u, v), outs))
    ]
    copies.append(pltpu.make_async_copy(depth, ints, sems.at[4]))
    for copy in copies:
        copy.start()
    copies[4].wait()
    h = ints[...].astype(jnp.float32)
    h_out[...] = h
    blank = jnp.zeros((3, LANES), jnp.float32)
    last = 4 * levels
    to_a[last : last + 4, :] = jnp.concatenate([jnp.where(even, h[7:8], h[0:1]), blank], axis=0)
    to_b[last : last + 4, :] = jnp.concatenate([jnp.where(even, h[0:1], h[7:8]), blank], axis=0)
    packed = []
    for f, ref in enumerate(outs):
        copies[f].wait()
        top = ref[pl.ds(ROWS - 1, levels, stride=ROWS), :]
        low = ref[pl.ds(0, levels, stride=ROWS), :]
        to_a[pl.ds(f, levels, stride=4), :] = jnp.where(even, top, low)
        b = jnp.where(even, low, top)
        to_b[pl.ds(f, levels, stride=4), :] = b
        packed.append(b)
    cu = level_to_lane(packed[2], LANES - 1)
    cv = level_to_lane(packed[3], 0)
    row = row_ids()
    corner[...] = jnp.where(row == 0, cu, jnp.where(row == 1, cv, 0.0))


def pack_columns(mesh_size, levels, early, t, s, u, v, depth, from_a, *refs):
    to_c, to_d = refs[-2:]
    lat, lon, first, _, _ = place_of(*mesh_size)
    lat_even = lax.rem(lat, 2) == 0
    lon_even = lax.rem(lon, 2) == 0
    if not early:

        @pl.when(first)
        def _():
            to_c[...] = refs[0][...]
            to_d[...] = refs[1][...]

    @pl.when(first if early else jnp.logical_not(first))
    def _():
        lane = lane_ids()
        h = depth[...]
        for f, ref in enumerate((t, s, u, v)):
            east = jnp.zeros((ROWS, LANES), jnp.float32)
            west = jnp.zeros((ROWS, LANES), jnp.float32)
            for k in range(levels):
                x = ref[k * ROWS : (k + 1) * ROWS, :]
                east = jnp.where(lane == k, roll(x, k + 1, 1), east)
                west = jnp.where(lane == k, roll(x, k, 1), west)
            if f == 0:
                east = jnp.where(lane == levels, h[:, LANES - 1 : LANES], east)
                west = jnp.where(lane == levels, h[:, 0:1], west)
            to_c[f * ROWS : (f + 1) * ROWS, :] = jnp.where(lon_even, east, west)
            to_d[f * ROWS : (f + 1) * ROWS, :] = jnp.where(lon_even, west, east)
        cu = level_to_lane(from_a[pl.ds(2, levels, stride=4), :], LANES - 1)
        cv = level_to_lane(from_a[pl.ds(3, levels, stride=4), :], 0)
        east = jnp.broadcast_to(jnp.where(lat_even, cu, 0.0), (ROWS, LANES))
        west = jnp.broadcast_to(jnp.where(lat_even, 0.0, cv), (ROWS, LANES))
        to_c[4 * ROWS : 5 * ROWS, :] = jnp.where(lon_even, east, west)
        to_d[4 * ROWS : 5 * ROWS, :] = jnp.where(lon_even, west, east)


def coriolis_rows(lat, total):
    row = (lat * ROWS + row_ids()).astype(jnp.float32)
    return CORIOLIS * (2.0 * (row + 0.5) / total - 1.0)


def local_work(mesh_size, levels, total, early, *refs):
    t, s, u, v, mix, depth = refs[:6]
    st, ss, su, sv, ra, aa, ba = refs[-7:]
    lat, _, _, soon, _ = place_of(*mesh_size)

    @pl.when(soon if early else jnp.logical_not(soon))
    def _():
        lane, row = lane_ids(), row_ids()
        h = depth[...]
        f4 = (0.25 * DT) * coriolis_rows(lat, total)
        open_e = jnp.where(lane < LANES - 1, jnp.minimum(h, roll(h, -1, 1)), 0.0)
        open_n = jnp.where(row < ROWS - 1, jnp.minimum(h, roll(h, -1, 0)), 0.0)
        zero = h - h
        one = zero + 1.0

        def level(k, carry):
            summed, c_here, minor, minor_prev = carry
            kf = jnp.asarray(k, jnp.float32)
            at = pl.ds(pl.multiple_of(k * ROWS, ROWS), ROWS)
            tk, sk, uk, vk = t[at, :], s[at, :], u[at, :], v[at, :]
            wet = h > kf
            dens = jnp.where(wet, PRESSURE * density_of(tk, sk), 0.0)
            summed = summed + dens
            p = summed - 0.5 * dens
            me, mn = open_e > kf, open_n > kf
            half_u, half_v = 0.5 * uk, 0.5 * vk
            e0, e1 = jnp.where(me, half_u + 0.5, 0.0), jnp.where(me, half_u - 0.5, 0.0)
            n0, n1 = jnp.where(mn, half_v + 0.5, 0.0), jnp.where(mn, half_v - 0.5, 0.0)
            for x, out in ((tk, st), (sk, ss)):
                fe = e0 * x + e1 * roll(x, -1, 1)
                fn = n0 * x + n1 * roll(x, -1, 0)
                out[k] = x - DT * (fe - roll(fe, 1, 1) + fn - roll(fn, 1, 0))
            uw, ve = roll(uk, 1, 1), roll(vk, -1, 1)
            un, vs = roll(uk, -1, 0), roll(vk, 1, 0)
            lap_u = (roll(uk, -1, 1) + uw) + (un + roll(uk, 1, 0)) - 4.0 * uk
            lap_v = (ve + roll(vk, 1, 1)) + (roll(vk, -1, 0) + vs) - 4.0 * vk
            v4 = (vk + ve) + (vs + roll(ve, 1, 0))
            u4 = (uk + uw) + (un + roll(uw, -1, 0))
            su[k] = uk + f4 * v4 - DT * (roll(p, -1, 1) - p) + 0.1 * lap_u
            sv[k] = vk - f4 * u4 - DT * (roll(p, -1, 0) - p) + 0.1 * lap_v
            below = mix[jnp.minimum(k, levels - 2)]
            c_next = jnp.where(h > kf + 1.0, DT * below, 0.0)
            minor_next = (1.0 + c_here + c_next) * minor - (c_here * c_here) * minor_prev
            r = jnp.where(wet, minor / minor_next, 0.0)
            ra[k] = r
            aa[k] = c_here * r
            ba[k] = c_next * r
            return summed, c_next, minor_next, minor

        lax.fori_loop(0, levels, level, (zero, zero, one, zero), unroll=UNROLL)


def finish(mesh_size, levels, total, *refs):
    (st, ss, su, sv, ra, aa, ba, depth, to_a, to_b, a_p, a_q, b_p, b_q, c_own, d_own,
     c_p, d_p, c_q, d_q, corner_p, corner_q, ot, os, ou, ov, north, south, kept) = refs
    lat, lon, first, _, top = place_of(*mesh_size)
    lane, row = lane_ids(), row_ids()
    lat_even = lax.rem(lat, 2) == 0
    lon_even = lax.rem(lon, 2) == 0
    k_first = jnp.logical_or(first, top)
    b_first = jnp.logical_or(k_first, together(lon, mesh_size[1]))
    h = depth[...]
    f4 = (0.25 * DT) * coriolis_rows(lat, total)
    f7, f0 = f4[7:8, :], f4[0:1, :]

    kk = lax.broadcasted_iota(jnp.int32, (levels, LANES), 0).astype(jnp.float32)
    ll = lax.broadcasted_iota(jnp.int32, (levels, LANES), 1)

    def field(ref, f):
        return ref[pl.ds(f, levels, stride=4), :]

    def ghosts(f):
        a = jnp.where(first, field(a_p, f), field(a_q, f))
        b = jnp.where(b_first, field(b_p, f), field(b_q, f))
        return jnp.where(lat_even, a, b), jnp.where(lat_even, b, a)

    def own(f):
        a, b = field(to_a, f), field(to_b, f)
        return jnp.where(lat_even, a, b), jnp.where(lat_even, b, a)

    def mirrored(x, last):
        ids = lax.rem(last + LANES - lax.broadcasted_iota(jnp.int32, x.shape, 1), LANES)
        return jnp.take_along_axis(x, ids, axis=1)

    at = slice(4 * levels, 4 * levels + 1)
    h_a = jnp.where(first, a_p[at, :], a_q[at, :])
    h_b = jnp.where(b_first, b_p[at, :], b_q[at, :])
    h_n = jnp.broadcast_to(jnp.where(lat_even, h_a, h_b), (ROWS, LANES))
    h_n = jnp.where(top, mirrored(h_n, LANES - 1), h_n)[0:1, :]
    h_s = jnp.where(lat_even, h_b, h_a)
    (tn, ts), (sn, ss_), (un, us), (vn, vs) = (ghosts(f) for f in range(4))
    (t7, t0), (s7, s0), (u7, u0), (v7, v0) = (own(f) for f in range(4))
    tn = jnp.where(top, mirrored(tn, LANES - 1), tn)
    sn = jnp.where(top, mirrored(sn, LANES - 1), sn)
    vn = jnp.where(top, -mirrored(vn, LANES - 1), vn)
    un = jnp.where(top, -mirrored(un, LANES - 2), un)
    unw = roll(un, 1, 1)
    unw = jnp.where(ll > 0, unw - roll(u0, 1, 1), jnp.where(top, unw, 0.0))
    un = jnp.where(jnp.logical_and(top, ll == LANES - 1), 0.0, un) - u0
    mask = jnp.minimum(h[7:8, :], h_n) > kk
    north[0, :levels, :] = jnp.where(mask, -0.1 * (v7 * (t7 + tn) - (tn - t7)), 0.0)
    north[1, :levels, :] = jnp.where(mask, -0.1 * (v7 * (s7 + sn) - (sn - s7)), 0.0)
    north[2, :levels, :] = 0.1 * un
    north[3, :levels, :] = 0.1 * (vn - v0) - f7 * (un + unw)
    north[4, :levels, :] = (DT * PRESSURE) * (
        jnp.where(h_n > kk, density_of(tn, sn), 0.0)
        - jnp.where(h[0:1, :] > kk, density_of(t0, s0), 0.0)
    )
    mask = jnp.minimum(h[0:1, :], h_s) > kk
    south[0, :levels, :] = jnp.where(mask, 0.1 * (vs * (ts + t0) - (t0 - ts)), 0.0)
    south[1, :levels, :] = jnp.where(mask, 0.1 * (vs * (ss_ + s0) - (s0 - ss_)), 0.0)
    vs = vs - v7
    vse = jnp.where(ll < LANES - 1, roll(vs, -1, 1), 0.0)
    south[2, :levels, :] = 0.1 * (us - u7) + f0 * (vs + vse)
    south[3, :levels, :] = 0.1 * vs

    kl = lane.astype(jnp.float32)

    def tiles(c, d, f):
        at = slice(f * ROWS, (f + 1) * ROWS)
        x, y = c(at), d(at)
        return jnp.where(lon_even, x, y), jnp.where(lon_even, y, x)

    def got_c(at):
        return jnp.where(first, c_p[at, :], c_q[at, :])

    def got_d(at):
        return jnp.where(first, d_p[at, :], d_q[at, :])

    def own_c(at):
        return c_own[at, :]

    def own_d(at):
        return d_own[at, :]

    (te, tw), (se, sw), (ue, uw), (ve, vw), (ce, cw) = (tiles(got_c, got_d, f) for f in range(5))
    (t9, tz), (s9, sz), (u9, uz), (v9, vz) = (tiles(own_c, own_d, f) for f in range(4))
    cb = jnp.where(k_first, corner_p[...], corner_q[...])
    cb_u = jnp.broadcast_to(cb[0:1, :], (ROWS, LANES))
    cb_v = jnp.broadcast_to(cb[1:2, :], (ROWS, LANES))
    south_east = jnp.where(lat_even, cb_v, ce)
    north_west = jnp.where(lat_even, cw, jnp.where(top, 0.0, cb_u))
    north_end = jnp.where(jnp.logical_and(top, row == ROWS - 1), -cb_u, 0.0)
    h_e = te[:, levels : levels + 1]
    h_w = tw[:, levels : levels + 1]
    mask = jnp.minimum(h[:, LANES - 1 : LANES], h_e) > kl
    dt_e = jnp.where(mask, -0.1 * (u9 * (t9 + te) - (te - t9)), 0.0)
    ds_e = jnp.where(mask, -0.1 * (u9 * (s9 + se) - (se - s9)), 0.0)
    mask = jnp.minimum(h[:, 0:1], h_w) > kl
    dt_w = jnp.where(mask, 0.1 * (uw * (tw + tz) - (tz - tw)), 0.0)
    ds_w = jnp.where(mask, 0.1 * (uw * (sw + sz) - (sz - sw)), 0.0)
    dens = jnp.where(h_e > kl, density_of(te, se), 0.0) - jnp.where(
        h[:, 0:1] > kl, density_of(tz, sz), 0.0
    )
    summed = dens
    for step in (1, 2, 4, 8, 16, 32, 64):
        summed = summed + jnp.where(lane >= step, roll(summed, step, 1), 0.0)
    pe = (DT * PRESSURE) * (summed - 0.5 * dens)
    ve_up = jnp.where(row > 0, roll(ve, 1, 0), south_east) - roll(vz, 1, 0)
    uw_dn = jnp.where(row < ROWS - 1, roll(uw, -1, 0), north_west) - roll(u9, -1, 0)
    du_e = f4 * ((ve - vz) + ve_up) - pe + 0.1 * (ue - uz) + 0.1 * north_end
    du_w = 0.1 * (uw - u9)
    dv_e = 0.1 * (ve - vz) - f4 * north_end
    dv_w = 0.1 * (vw - v9) - f4 * ((uw - u9) + uw_dn)

    m_u = jnp.minimum(h, jnp.where(lane < LANES - 1, roll(h, -1, 1), h_e))
    m_v = jnp.minimum(h, jnp.where(row < ROWS - 1, roll(h, -1, 0), h_n))
    at_n, at_s = row == ROWS - 1, row == 0
    at_e, at_w = lane == LANES - 1, lane == 0
    inner, last = elimination_constants(levels)
    sides = ((dt_e, dt_w), (ds_e, ds_w), (du_e, du_w), (dv_e, dv_w))

    def down(k, c, carry):
        pt, ps, pu, pv, cs = carry
        kf = jnp.asarray(k, jnp.float32)
        one = pl.ds(k, 1)

        def spread(f, extra=None):
            n = north[f, one, :]
            if extra is not None:
                n = n - extra
            base = jnp.where(at_n, n, jnp.where(at_s, south[f, one, :], 0.0))
            de = pltpu.roll(sides[f][0], LANES - 1 - k, 1)
            dw = pltpu.roll(sides[f][1], (LANES - k) % LANES, 1)
            return base + jnp.where(at_e, de, jnp.where(at_w, dw, 0.0))

        dn = north[4, one, :]
        cs = cs + dn
        r, a = ra[k], aa[k]
        ru = jnp.where(m_u > kf + 1.0, inner[c], jnp.where(m_u > kf, last[c], 0.0))
        rv = jnp.where(m_v > kf + 1.0, inner[c], jnp.where(m_v > kf, last[c], 0.0))
        pt = r * (st[k] + spread(0)) + a * pt
        ps = r * (ss[k] + spread(1)) + a * ps
        pu = ru * (su[k] + spread(2)) + (VISC_STEP * ru) * pu
        pv = rv * (sv[k] + spread(3, cs - 0.5 * dn)) + (VISC_STEP * rv) * pv
        for f, x in enumerate((pt, ps, pu, pv)):
            kept[f, k] = x
        return pt, ps, pu, pv, cs

    def up(k, c, carry):
        xt, xs, xu, xv = carry
        kf = jnp.asarray(k, jnp.float32)
        b = ba[k]
        bu = jnp.where(m_u > kf + 1.0, VISC_STEP * inner[c], 0.0)
        bv = jnp.where(m_v > kf + 1.0, VISC_STEP * inner[c], 0.0)
        xt = kept[0, k] + b * xt
        xs = kept[1, k] + b * xs
        xu = kept[2, k] + bu * xu
        xv = kept[3, k] + bv * xv
        ot[k], os[k], ou[k], ov[k] = xt, xs, xu, xv
        return xt, xs, xu, xv

    zero = h - h
    carry = (zero, zero, zero, zero, zero[0:1, :])
    for k in range(levels):
        carry = down(k, k, carry)
    carry = (zero,) * 4
    for k in range(levels - 1, -1, -1):
        carry = up(k, k, carry)


HBM = pl.BlockSpec(memory_space=pltpu.HBM)
VMEM = pl.BlockSpec(memory_space=pltpu.VMEM)


def call(body, far, near, outs, scratch=(), aliases=None, keep=True):
    far = [pltpu.with_memory_space_constraint(x, pltpu.HBM) for x in far]
    near = [pltpu.with_memory_space_constraint(x, pltpu.VMEM) for x in near]
    shapes = tuple(
        pltpu.VMEM(s, jnp.float32) if keep else jax.ShapeDtypeStruct(s, jnp.float32) for s in outs
    )
    return pl.pallas_call(
        body,
        out_shape=shapes,
        in_specs=[HBM] * len(far) + [VMEM] * len(near),
        out_specs=tuple(VMEM for _ in outs),
        scratch_shapes=list(scratch),
        input_output_aliases=aliases or {},
        compiler_params=pltpu.CompilerParams(vmem_limit_bytes=VMEM_GRANT),
    )(*far, *near)


def together(lon, n_lon):
    return (lon >= n_lon // 2) & (lon < n_lon * 7 // 8)


def exchanges(n_lat, n_lon):
    def at(lat, lon):
        return (lon % n_lon) * n_lat + lat

    def both(x, y):
        return [(x, y), (y, x)]

    p = {name: [] for name in [x + y for x in "abkcd" for y in ("_p", "_q")]}
    for lon in range(n_lon):
        for lat in range(0, n_lat, 2):
            p["a_p" if lat % 4 < 2 else "a_q"] += both(at(lat, lon), at(lat + 1, lon))
        for lat in range(1, n_lat - 1, 2):
            for x, y in both((lat, lon), (lat + 1, lon)):
                now = y[0] % 4 < 2 or together(lon, n_lon)
                p["b_p" if now else "b_q"].append((at(*x), at(*y)))
            for x, y in both((lat, lon), (lat + 1, lon - 1)):
                p["k_p" if y[0] % 4 < 2 else "k_q"].append((at(*x), at(*y)))
        p["b_p"].append((at(n_lat - 1, lon), at(n_lat - 1, n_lon - 1 - lon)))
        p["k_p"].append((at(n_lat - 1, lon), at(n_lat - 1, n_lon - 2 - lon)))
    for lat in range(n_lat):
        side = "p" if lat % 4 < 2 else "q"
        for lon in range(0, n_lon, 2):
            p["c_" + side] += both(at(lat, lon), at(lat, lon + 1))
            p["d_" + side] += both(at(lat, lon + 1), at(lat, lon + 2))
    return p


def local(t, s, u, v, mix, depth):
    levels = t.shape[0]
    size = (lax.axis_size("lat"), lax.axis_size("lon"))
    total = float(size[0] * ROWS)
    pairs = exchanges(*size)
    flat = (levels * ROWS, LANES)
    rows, full = (4 * levels + 4, LANES), (levels, ROWS, LANES)
    column = (COL_ROWS, LANES)

    def send(x, name):
        return lax.ppermute(x, ("lon", "lat"), pairs[name])

    def bind(body, *args):
        return lambda *refs: body(size, levels, *args, *refs)

    *fields, depth, to_a, to_b, to_corner = call(
        bind(pack_rows), [x.reshape(flat) for x in (t, s, u, v)] + [depth], [],
        [flat] * 4 + [(ROWS, LANES), rows, rows, (ROWS, LANES)],
        [pltpu.VMEM((ROWS, LANES), jnp.int32), pltpu.SemaphoreType.DMA((5,))],
    )
    b_p = send(to_b, "b_p")
    k_p = send(to_corner, "k_p")
    a_p = send(to_a, "a_p")
    cols_p = call(bind(pack_columns, True), [], [*fields, depth, a_p], [column] * 2)
    d_p = send(cols_p[1], "d_p")
    c_p = send(cols_p[0], "c_p")
    work = call(bind(local_work, total, True), [], [*fields, mix, depth], [full] * 7)
    b_q = send(to_b, "b_q")
    k_q = send(to_corner, "k_q")
    a_q = send(to_a, "a_q")
    cols_q = call(bind(pack_columns, False), [], [*fields, depth, a_q, *cols_p], [column] * 2)
    d_q = send(cols_q[1], "d_q")
    c_q = send(cols_q[0], "c_q")
    work = call(
        bind(local_work, total, False), [], [*fields, mix, depth, *work], [full] * 7,
        aliases={6 + i: i for i in range(7)},
    )
    padded = (levels + 7) // 8 * 8
    return tuple(
        call(
            bind(finish, total), [],
            [*work, depth, to_a, to_b, a_p, a_q, b_p, b_q, *cols_q, c_p, d_p, c_q, d_q, k_p, k_q],
            [full] * 4,
            [
                pltpu.VMEM((5, padded, LANES), jnp.float32),
                pltpu.VMEM((4, padded, LANES), jnp.float32),
                pltpu.VMEM((4,) + full, jnp.float32),
            ],
            keep=False,
        )
    )


def solution(mesh):
    field = P(None, "lat", "lon")

    return jax.shard_map(
        local,
        mesh=mesh,
        in_specs=(field,) * 5 + (P("lat", "lon"),),
        out_specs=(field,) * 4,
        check_vma=False,
    )
```

```python
import jax
import jax.numpy as jnp
from jax import lax
from jax.experimental import pallas as pl
from jax.experimental.pallas import tpu as pltpu
from jax.sharding import PartitionSpec as P


DT = 0.2
CORIOLIS = 1.5
PRESSURE = 0.05
VISC_STEP = 0.1

ROWS, LANES = 8, 128
VMEM_GRANT = 8 << 20
UNROLL = 5
COL_ROWS = 40


def elimination_constants(levels):
    inner, last = [], []
    for k in range(levels):
        above = VISC_STEP * VISC_STEP * inner[k - 1] if k else 0.0
        step = VISC_STEP if k else 0.0
        inner.append(1.0 / (1.0 + step + VISC_STEP - above))
        last.append(1.0 / (1.0 + step - above))
    return inner, last


def lane_ids():
    return lax.broadcasted_iota(jnp.int32, (ROWS, LANES), 1)


def row_ids():
    return lax.broadcasted_iota(jnp.int32, (ROWS, LANES), 0)


def roll(x, shift, axis):
    return pltpu.roll(x, shift % x.shape[axis], axis)


def density_of(t, s):
    return -(1.0 + 0.1 * t) * t + 0.8 * s - 0.1 * t * s


def level_to_lane(rows, lane):
    k = lax.broadcasted_iota(jnp.int32, rows.shape, 0)
    l = lax.broadcasted_iota(jnp.int32, rows.shape, 1)
    return jnp.sum(jnp.where(k == l, rows[:, lane : lane + 1], 0.0), axis=0, keepdims=True)


def place_of(n_lat, n_lon):
    lat, lon = lax.axis_index("lat"), lax.axis_index("lon")
    first = lax.rem(lat, 4) < 2
    return lat, lon, first, jnp.logical_and(first, lon < n_lon // 2), lat == n_lat - 1


def pack_rows(mesh_size, levels, t, s, u, v, depth, t_out, s_out, u_out, v_out, h_out, to_a, to_b, corner, ints, sems):
    lat, _, _, _, _ = place_of(*mesh_size)
    even = lax.rem(lat, 2) == 0
    outs = (t_out, s_out, u_out, v_out)
    copies = [
        pltpu.make_async_copy(x, y, sems.at[f]) for f, (x, y) in enumerate(zip((t, s, u, v), outs))
    ]
    copies.append(pltpu.make_async_copy(depth, ints, sems.at[4]))
    for copy in copies:
        copy.start()
    copies[4].wait()
    h = ints[...].astype(jnp.float32)
    h_out[...] = h
    blank = jnp.zeros((3, LANES), jnp.float32)
    last = 4 * levels
    to_a[last : last + 4, :] = jnp.concatenate([jnp.where(even, h[7:8], h[0:1]), blank], axis=0)
    to_b[last : last + 4, :] = jnp.concatenate([jnp.where(even, h[0:1], h[7:8]), blank], axis=0)
    packed = []
    for f, ref in enumerate(outs):
        copies[f].wait()
        top = ref[pl.ds(ROWS - 1, levels, stride=ROWS), :]
        low = ref[pl.ds(0, levels, stride=ROWS), :]
        to_a[pl.ds(f, levels, stride=4), :] = jnp.where(even, top, low)
        b = jnp.where(even, low, top)
        to_b[pl.ds(f, levels, stride=4), :] = b
        packed.append(b)
    cu = level_to_lane(packed[2], LANES - 1)
    cv = level_to_lane(packed[3], 0)
    row = row_ids()
    corner[...] = jnp.where(row == 0, cu, jnp.where(row == 1, cv, 0.0))


def pack_columns(mesh_size, levels, early, t, s, u, v, depth, from_a, *refs):
    to_c, to_d = refs[-2:]
    lat, lon, first, _, _ = place_of(*mesh_size)
    lat_even = lax.rem(lat, 2) == 0
    lon_even = lax.rem(lon, 2) == 0
    if not early:

        @pl.when(first)
        def _():
            to_c[...] = refs[0][...]
            to_d[...] = refs[1][...]

    @pl.when(first if early else jnp.logical_not(first))
    def _():
        lane = lane_ids()
        h = depth[...]
        for f, ref in enumerate((t, s, u, v)):
            east = jnp.zeros((ROWS, LANES), jnp.float32)
            west = jnp.zeros((ROWS, LANES), jnp.float32)
            for k in range(levels):
                x = ref[k * ROWS : (k + 1) * ROWS, :]
                east = jnp.where(lane == k, roll(x, k + 1, 1), east)
                west = jnp.where(lane == k, roll(x, k, 1), west)
            if f == 0:
                east = jnp.where(lane == levels, h[:, LANES - 1 : LANES], east)
                west = jnp.where(lane == levels, h[:, 0:1], west)
            to_c[f * ROWS : (f + 1) * ROWS, :] = jnp.where(lon_even, east, west)
            to_d[f * ROWS : (f + 1) * ROWS, :] = jnp.where(lon_even, west, east)
        cu = level_to_lane(from_a[pl.ds(2, levels, stride=4), :], LANES - 1)
        cv = level_to_lane(from_a[pl.ds(3, levels, stride=4), :], 0)
        east = jnp.broadcast_to(jnp.where(lat_even, cu, 0.0), (ROWS, LANES))
        west = jnp.broadcast_to(jnp.where(lat_even, 0.0, cv), (ROWS, LANES))
        to_c[4 * ROWS : 5 * ROWS, :] = jnp.where(lon_even, east, west)
        to_d[4 * ROWS : 5 * ROWS, :] = jnp.where(lon_even, west, east)


def coriolis_rows(lat, total):
    row = (lat * ROWS + row_ids()).astype(jnp.float32)
    return CORIOLIS * (2.0 * (row + 0.5) / total - 1.0)


def local_work(mesh_size, levels, total, early, *refs):
    t, s, u, v, mix, depth = refs[:6]
    st, ss, su, sv, ra, aa, ba = refs[-7:]
    lat, _, _, soon, _ = place_of(*mesh_size)

    @pl.when(soon if early else jnp.logical_not(soon))
    def _():
        lane, row = lane_ids(), row_ids()
        h = depth[...]
        f4 = (0.25 * DT) * coriolis_rows(lat, total)
        open_e = jnp.where(lane < LANES - 1, jnp.minimum(h, roll(h, -1, 1)), 0.0)
        open_n = jnp.where(row < ROWS - 1, jnp.minimum(h, roll(h, -1, 0)), 0.0)
        zero = h - h
        one = zero + 1.0

        def level(k, carry):
            summed, c_here, minor, minor_prev = carry
            kf = jnp.asarray(k, jnp.float32)
            at = pl.ds(pl.multiple_of(k * ROWS, ROWS), ROWS)
            tk, sk, uk, vk = t[at, :], s[at, :], u[at, :], v[at, :]
            wet = h > kf
            dens = jnp.where(wet, PRESSURE * density_of(tk, sk), 0.0)
            summed = summed + dens
            p = summed - 0.5 * dens
            me, mn = open_e > kf, open_n > kf
            half_u, half_v = 0.5 * uk, 0.5 * vk
            e0, e1 = jnp.where(me, half_u + 0.5, 0.0), jnp.where(me, half_u - 0.5, 0.0)
            n0, n1 = jnp.where(mn, half_v + 0.5, 0.0), jnp.where(mn, half_v - 0.5, 0.0)
            for x, out in ((tk, st), (sk, ss)):
                fe = e0 * x + e1 * roll(x, -1, 1)
                fn = n0 * x + n1 * roll(x, -1, 0)
                out[k] = x - DT * (fe - roll(fe, 1, 1) + fn - roll(fn, 1, 0))
            uw, ve = roll(uk, 1, 1), roll(vk, -1, 1)
            un, vs = roll(uk, -1, 0), roll(vk, 1, 0)
            lap_u = (roll(uk, -1, 1) + uw) + (un + roll(uk, 1, 0)) - 4.0 * uk
            lap_v = (ve + roll(vk, 1, 1)) + (roll(vk, -1, 0) + vs) - 4.0 * vk
            v4 = (vk + ve) + (vs + roll(ve, 1, 0))
            u4 = (uk + uw) + (un + roll(uw, -1, 0))
            su[k] = uk + f4 * v4 - DT * (roll(p, -1, 1) - p) + 0.1 * lap_u
            sv[k] = vk - f4 * u4 - DT * (roll(p, -1, 0) - p) + 0.1 * lap_v
            below = mix[jnp.minimum(k, levels - 2)]
            c_next = jnp.where(h > kf + 1.0, DT * below, 0.0)
            minor_next = (1.0 + c_here + c_next) * minor - (c_here * c_here) * minor_prev
            r = jnp.where(wet, minor / minor_next, 0.0)
            ra[k] = r
            aa[k] = c_here * r
            ba[k] = c_next * r
            return summed, c_next, minor_next, minor

        lax.fori_loop(0, levels, level, (zero, zero, one, zero), unroll=UNROLL)


def finish(mesh_size, levels, total, *refs):
    (st, ss, su, sv, ra, aa, ba, depth, to_a, to_b, a_p, a_q, b_p, b_q, c_own, d_own,
     c_p, d_p, c_q, d_q, corner_p, corner_q, ot, os, ou, ov, north, south, kept) = refs
    lat, lon, first, _, top = place_of(*mesh_size)
    lane, row = lane_ids(), row_ids()
    lat_even = lax.rem(lat, 2) == 0
    lon_even = lax.rem(lon, 2) == 0
    k_first = jnp.logical_or(first, top)
    b_first = jnp.logical_or(k_first, together(lon, mesh_size[1]))
    h = depth[...]
    f4 = (0.25 * DT) * coriolis_rows(lat, total)
    f7, f0 = f4[7:8, :], f4[0:1, :]

    kk = lax.broadcasted_iota(jnp.int32, (levels, LANES), 0).astype(jnp.float32)
    ll = lax.broadcasted_iota(jnp.int32, (levels, LANES), 1)

    def field(ref, f):
        return ref[pl.ds(f, levels, stride=4), :]

    def ghosts(f):
        a = jnp.where(first, field(a_p, f), field(a_q, f))
        b = jnp.where(b_first, field(b_p, f), field(b_q, f))
        return jnp.where(lat_even, a, b), jnp.where(lat_even, b, a)

    def own(f):
        a, b = field(to_a, f), field(to_b, f)
        return jnp.where(lat_even, a, b), jnp.where(lat_even, b, a)

    def mirrored(x, last):
        ids = lax.rem(last + LANES - lax.broadcasted_iota(jnp.int32, x.shape, 1), LANES)
        return jnp.take_along_axis(x, ids, axis=1)

    at = slice(4 * levels, 4 * levels + 1)
    h_a = jnp.where(first, a_p[at, :], a_q[at, :])
    h_b = jnp.where(b_first, b_p[at, :], b_q[at, :])
    h_n = jnp.broadcast_to(jnp.where(lat_even, h_a, h_b), (ROWS, LANES))
    h_n = jnp.where(top, mirrored(h_n, LANES - 1), h_n)[0:1, :]
    h_s = jnp.where(lat_even, h_b, h_a)
    (tn, ts), (sn, ss_), (un, us), (vn, vs) = (ghosts(f) for f in range(4))
    (t7, t0), (s7, s0), (u7, u0), (v7, v0) = (own(f) for f in range(4))
    tn = jnp.where(top, mirrored(tn, LANES - 1), tn)
    sn = jnp.where(top, mirrored(sn, LANES - 1), sn)
    vn = jnp.where(top, -mirrored(vn, LANES - 1), vn)
    un = jnp.where(top, -mirrored(un, LANES - 2), un)
    unw = roll(un, 1, 1)
    unw = jnp.where(ll > 0, unw - roll(u0, 1, 1), jnp.where(top, unw, 0.0))
    un = jnp.where(jnp.logical_and(top, ll == LANES - 1), 0.0, un) - u0
    mask = jnp.minimum(h[7:8, :], h_n) > kk
    north[0, :levels, :] = jnp.where(mask, -0.1 * (v7 * (t7 + tn) - (tn - t7)), 0.0)
    north[1, :levels, :] = jnp.where(mask, -0.1 * (v7 * (s7 + sn) - (sn - s7)), 0.0)
    north[2, :levels, :] = 0.1 * un
    north[3, :levels, :] = 0.1 * (vn - v0) - f7 * (un + unw)
    north[4, :levels, :] = (DT * PRESSURE) * (
        jnp.where(h_n > kk, density_of(tn, sn), 0.0)
        - jnp.where(h[0:1, :] > kk, density_of(t0, s0), 0.0)
    )
    mask = jnp.minimum(h[0:1, :], h_s) > kk
    south[0, :levels, :] = jnp.where(mask, 0.1 * (vs * (ts + t0) - (t0 - ts)), 0.0)
    south[1, :levels, :] = jnp.where(mask, 0.1 * (vs * (ss_ + s0) - (s0 - ss_)), 0.0)
    vs = vs - v7
    vse = jnp.where(ll < LANES - 1, roll(vs, -1, 1), 0.0)
    south[2, :levels, :] = 0.1 * (us - u7) + f0 * (vs + vse)
    south[3, :levels, :] = 0.1 * vs

    kl = lane.astype(jnp.float32)

    def tiles(c, d, f):
        at = slice(f * ROWS, (f + 1) * ROWS)
        x, y = c(at), d(at)
        return jnp.where(lon_even, x, y), jnp.where(lon_even, y, x)

    def got_c(at):
        return jnp.where(first, c_p[at, :], c_q[at, :])

    def got_d(at):
        return d_p[at, :] + d_q[at, :]

    def own_c(at):
        return c_own[at, :]

    def own_d(at):
        return d_own[at, :]

    (te, tw), (se, sw), (ue, uw), (ve, vw), (ce, cw) = (tiles(got_c, got_d, f) for f in range(5))
    (t9, tz), (s9, sz), (u9, uz), (v9, vz) = (tiles(own_c, own_d, f) for f in range(4))
    cb = jnp.where(k_first, corner_p[...], corner_q[...])
    cb_u = jnp.broadcast_to(cb[0:1, :], (ROWS, LANES))
    cb_v = jnp.broadcast_to(cb[1:2, :], (ROWS, LANES))
    south_east = jnp.where(lat_even, cb_v, ce)
    north_west = jnp.where(lat_even, cw, jnp.where(top, 0.0, cb_u))
    north_end = jnp.where(jnp.logical_and(top, row == ROWS - 1), -cb_u, 0.0)
    h_e = te[:, levels : levels + 1]
    h_w = tw[:, levels : levels + 1]
    mask = jnp.minimum(h[:, LANES - 1 : LANES], h_e) > kl
    dt_e = jnp.where(mask, -0.1 * (u9 * (t9 + te) - (te - t9)), 0.0)
    ds_e = jnp.where(mask, -0.1 * (u9 * (s9 + se) - (se - s9)), 0.0)
    mask = jnp.minimum(h[:, 0:1], h_w) > kl
    dt_w = jnp.where(mask, 0.1 * (uw * (tw + tz) - (tz - tw)), 0.0)
    ds_w = jnp.where(mask, 0.1 * (uw * (sw + sz) - (sz - sw)), 0.0)
    dens = jnp.where(h_e > kl, density_of(te, se), 0.0) - jnp.where(
        h[:, 0:1] > kl, density_of(tz, sz), 0.0
    )
    summed = dens
    for step in (1, 2, 4, 8, 16, 32, 64):
        summed = summed + jnp.where(lane >= step, roll(summed, step, 1), 0.0)
    pe = (DT * PRESSURE) * (summed - 0.5 * dens)
    ve_up = jnp.where(row > 0, roll(ve, 1, 0), south_east) - roll(vz, 1, 0)
    uw_dn = jnp.where(row < ROWS - 1, roll(uw, -1, 0), north_west) - roll(u9, -1, 0)
    du_e = f4 * ((ve - vz) + ve_up) - pe + 0.1 * (ue - uz) + 0.1 * north_end
    du_w = 0.1 * (uw - u9)
    dv_e = 0.1 * (ve - vz) - f4 * north_end
    dv_w = 0.1 * (vw - v9) - f4 * ((uw - u9) + uw_dn)

    m_u = jnp.minimum(h, jnp.where(lane < LANES - 1, roll(h, -1, 1), h_e))
    m_v = jnp.minimum(h, jnp.where(row < ROWS - 1, roll(h, -1, 0), h_n))
    at_n, at_s = row == ROWS - 1, row == 0
    at_e, at_w = lane == LANES - 1, lane == 0
    inner, last = elimination_constants(levels)
    sides = ((dt_e, dt_w), (ds_e, ds_w), (du_e, du_w), (dv_e, dv_w))

    def down(k, c, carry):
        pt, ps, pu, pv, cs = carry
        kf = jnp.asarray(k, jnp.float32)
        one = pl.ds(k, 1)

        def spread(f, extra=None):
            n = north[f, one, :]
            if extra is not None:
                n = n - extra
            base = jnp.where(at_n, n, jnp.where(at_s, south[f, one, :], 0.0))
            de = pltpu.roll(sides[f][0], LANES - 1 - k, 1)
            dw = pltpu.roll(sides[f][1], (LANES - k) % LANES, 1)
            return base + jnp.where(at_e, de, jnp.where(at_w, dw, 0.0))

        dn = north[4, one, :]
        cs = cs + dn
        r, a = ra[k], aa[k]
        ru = jnp.where(m_u > kf + 1.0, inner[c], jnp.where(m_u > kf, last[c], 0.0))
        rv = jnp.where(m_v > kf + 1.0, inner[c], jnp.where(m_v > kf, last[c], 0.0))
        pt = r * (st[k] + spread(0)) + a * pt
        ps = r * (ss[k] + spread(1)) + a * ps
        pu = ru * (su[k] + spread(2)) + (VISC_STEP * ru) * pu
        pv = rv * (sv[k] + spread(3, cs - 0.5 * dn)) + (VISC_STEP * rv) * pv
        for f, x in enumerate((pt, ps, pu, pv)):
            kept[f, k] = x
        return pt, ps, pu, pv, cs

    def up(k, c, carry):
        xt, xs, xu, xv = carry
        kf = jnp.asarray(k, jnp.float32)
        b = ba[k]
        bu = jnp.where(m_u > kf + 1.0, VISC_STEP * inner[c], 0.0)
        bv = jnp.where(m_v > kf + 1.0, VISC_STEP * inner[c], 0.0)
        xt = kept[0, k] + b * xt
        xs = kept[1, k] + b * xs
        xu = kept[2, k] + bu * xu
        xv = kept[3, k] + bv * xv
        ot[k], os[k], ou[k], ov[k] = xt, xs, xu, xv
        return xt, xs, xu, xv

    zero = h - h
    carry = (zero, zero, zero, zero, zero[0:1, :])
    for k in range(levels):
        carry = down(k, k, carry)
    carry = (zero,) * 4
    for k in range(levels - 1, -1, -1):
        carry = up(k, k, carry)


HBM = pl.BlockSpec(memory_space=pltpu.HBM)
VMEM = pl.BlockSpec(memory_space=pltpu.VMEM)


def call(body, far, near, outs, scratch=(), aliases=None, keep=True):
    far = [pltpu.with_memory_space_constraint(x, pltpu.HBM) for x in far]
    near = [pltpu.with_memory_space_constraint(x, pltpu.VMEM) for x in near]
    shapes = tuple(
        pltpu.VMEM(s, jnp.float32) if keep else jax.ShapeDtypeStruct(s, jnp.float32) for s in outs
    )
    return pl.pallas_call(
        body,
        out_shape=shapes,
        in_specs=[HBM] * len(far) + [VMEM] * len(near),
        out_specs=tuple(VMEM for _ in outs),
        scratch_shapes=list(scratch),
        input_output_aliases=aliases or {},
        compiler_params=pltpu.CompilerParams(vmem_limit_bytes=VMEM_GRANT),
    )(*far, *near)


def together(lon, n_lon):
    return (lon >= n_lon * 5 // 8) & (lon < n_lon * 7 // 8)


def exchanges(n_lat, n_lon):
    def at(lat, lon):
        return (lon % n_lon) * n_lat + lat

    def both(x, y):
        return [(x, y), (y, x)]

    p = {name: [] for name in [x + y for x in "abkcd" for y in ("_p", "_q")]}
    for lon in range(n_lon):
        for lat in range(0, n_lat, 2):
            p["a_p" if lat % 4 < 2 else "a_q"] += both(at(lat, lon), at(lat + 1, lon))
        for lat in range(1, n_lat - 1, 2):
            for x, y in both((lat, lon), (lat + 1, lon)):
                now = y[0] % 4 < 2 or together(lon, n_lon)
                p["b_p" if now else "b_q"].append((at(*x), at(*y)))
            for x, y in both((lat, lon), (lat + 1, lon - 1)):
                p["k_p" if y[0] % 4 < 2 else "k_q"].append((at(*x), at(*y)))
        p["b_p"].append((at(n_lat - 1, lon), at(n_lat - 1, n_lon - 1 - lon)))
        p["k_p"].append((at(n_lat - 1, lon), at(n_lat - 1, n_lon - 2 - lon)))
    for lat in range(n_lat):
        side = "p" if lat % 4 < 2 else "q"
        for lon in range(0, n_lon, 2):
            p["c_" + side] += both(at(lat, lon), at(lat, lon + 1))
            edge = together(lon + 1, n_lon) != together((lon + 2) % n_lon, n_lon)
            p["d_q" if edge else "d_" + side] += both(at(lat, lon + 1), at(lat, lon + 2))
    return p


def local(t, s, u, v, mix, depth):
    levels = t.shape[0]
    size = (lax.axis_size("lat"), lax.axis_size("lon"))
    total = float(size[0] * ROWS)
    pairs = exchanges(*size)
    flat = (levels * ROWS, LANES)
    rows, full = (4 * levels + 4, LANES), (levels, ROWS, LANES)
    column = (COL_ROWS, LANES)

    def send(x, name):
        return lax.ppermute(x, ("lon", "lat"), pairs[name])

    def bind(body, *args):
        return lambda *refs: body(size, levels, *args, *refs)

    *fields, depth, to_a, to_b, to_corner = call(
        bind(pack_rows), [x.reshape(flat) for x in (t, s, u, v)] + [depth], [],
        [flat] * 4 + [(ROWS, LANES), rows, rows, (ROWS, LANES)],
        [pltpu.VMEM((ROWS, LANES), jnp.int32), pltpu.SemaphoreType.DMA((5,))],
    )
    b_p = send(to_b, "b_p")
    k_p = send(to_corner, "k_p")
    a_p = send(to_a, "a_p")
    cols_p = call(bind(pack_columns, True), [], [*fields, depth, a_p], [column] * 2)
    d_p = send(cols_p[1], "d_p")
    c_p = send(cols_p[0], "c_p")
    work = call(bind(local_work, total, True), [], [*fields, mix, depth], [full] * 7)
    b_q = send(to_b, "b_q")
    k_q = send(to_corner, "k_q")
    a_q = send(to_a, "a_q")
    cols_q = call(bind(pack_columns, False), [], [*fields, depth, a_q, *cols_p], [column] * 2)
    d_q = send(cols_q[1], "d_q")
    c_q = send(cols_q[0], "c_q")
    work = call(
        bind(local_work, total, False), [], [*fields, mix, depth, *work], [full] * 7,
        aliases={6 + i: i for i in range(7)},
    )
    padded = (levels + 7) // 8 * 8
    return tuple(
        call(
            bind(finish, total), [],
            [*work, depth, to_a, to_b, a_p, a_q, b_p, b_q, *cols_q, c_p, d_p, c_q, d_q, k_p, k_q],
            [full] * 4,
            [
                pltpu.VMEM((5, padded, LANES), jnp.float32),
                pltpu.VMEM((4, padded, LANES), jnp.float32),
                pltpu.VMEM((4,) + full, jnp.float32),
            ],
            keep=False,
        )
    )


def solution(mesh):
    field = P(None, "lat", "lon")

    return jax.shard_map(
        local,
        mesh=mesh,
        in_specs=(field,) * 5 + (P("lat", "lon"),),
        out_specs=(field,) * 4,
        check_vma=False,
    )
```
